512 devices in a mesh: row: 64 (over z, y_hi, x), col: 8 (over y_lo, core).
Axes of the slice: x: 4, y: 8 (y_hi: 2, y_lo: 4; y = y_hi * 4 + y_lo), z: 8, core: 2. Of those that a mesh axis runs over, the one named last changes fastest.
Arguments:
- features: bfloat16 [128, 16384], P('col', 'row'), may hold values from -6 to 6
- order: int32 [16384], P('row'), may hold values from 0 to 16383, as said below
- weight: bfloat16 [128, 256], P(None, 'col'), may hold values from -0.5 to 0.5
- bias: bfloat16 [256], P('col'), may hold values from -3 to 3
- tiles: bfloat16 [128, 64, 128, 128], P('row'), may hold values from -0.09375 to 0.09375
- coords: int32 [128, 64], P('row'), may hold values from 0 to 127
- counts: int32 [128], P('row'), may hold values from 1 to 64, 4096 in all
- grad_hidden: bfloat16 [256, 16384], P('col', 'row'), may hold values from -6 to 6
Outputs:
- hidden: bfloat16 [256, 16384], P('col', 'row')
- grad_features: float32 [128, 16384], P('col', 'row')
- grad_weight: float32 [128, 256], P(None, 'col')
- grad_bias: float32 [256], P('col')
The draws below stay inside these ranges and needn't reach their ends.
Inputs may be any that keep to these rules, and one draw needn't show every extreme that they name: Within each aligned block of 256 nodes, order is a permutation of that block's node indices. `counts`: some block row fills all 64 slots. `coords`: slots of one block row may name the same column block.
All inputs are finite; a program needn't handle non-finite values.
Results may differ from the reference program's by a relative error of at most 0.0015.
Values may be sent and summed in bfloat16 or wider, within the bound.
No kernel may reach another device: no remote copies, remote signals or barrier semaphores. Data moves between devices by JAX's collectives and lax.ppermute only.
A program may use at most 64 MiB of HBM per device.

```python
import math
import jax
import jax.numpy as jnp
import numpy as np
from jax import lax

FIN = 128
HID = 256
TILE = 128
K = 64
BR_DEV = 2
BLOCKS = 128
ROWS_DEV = 256
NODES = 16384


def draw_order(key, part):
    groups = BLOCKS // BR_DEV
    sub_keys = jax.random.split(key, groups)
    shuffled = jax.vmap(lambda one_key: jax.random.permutation(one_key, ROWS_DEV))(sub_keys)
    offsets = jnp.arange(groups, dtype=jnp.int32)[:, None] * ROWS_DEV
    return (shuffled.astype(jnp.int32) + offsets).reshape(-1)


def touch_ends(array, key, low, top_value):
    place = [jax.random.randint(jax.random.fold_in(key, axis), (), 0, length) for axis, length in enumerate(array.shape)]
    main_axis = array.shape.index(max(array.shape))
    beside = place[:main_axis] + [(place[main_axis] + 1) % array.shape[main_axis]] + place[main_axis + 1:]
    return array.at[tuple(place)].set(low).at[tuple(beside)].set(top_value)


def level_of(own_key, extent, cuts, low, top_value):
    loudness, own = 1.0, jax.random.fold_in(own_key, 6)
    for axis_at, shards_of in cuts:
        heights = jnp.exp(jax.random.uniform(jax.random.fold_in(own, axis_at), (shards_of,), jnp.float32, low / len(cuts), top_value / len(cuts)))
        loudness = loudness * jnp.repeat(heights, extent[axis_at] // shards_of).reshape([-1 if axis == axis_at else 1 for axis in range(len(extent))])
    return loudness


def split_up(count, total, most, lean):
    weights = [(1 << 20) // math.isqrt(rank ** lean) + 1 for rank in range(2, count + 1)]
    surplus, given = total - most - (count - 1), [1] * (count - 1)
    while surplus > 0:
        free = [i for i in range(count - 1) if given[i] < most]
        mass, budget = sum([weights[i] for i in free]), surplus
        for i in free:
            more = min(most - given[i], max(1, budget * weights[i] // mass), surplus)
            given[i] = given[i] + more
            surplus = surplus - more
    return np.array([most] + given)


def ragged(rng, amount, total, most, slope):
    if amount == 2:
        one = jax.random.randint(rng, (), max(1, total - most), min(most, total - 1) + 1)
        return jnp.stack([one, total - one])
    lengths = jnp.asarray(split_up(amount, total, most, slope), jnp.int32)
    couples = (amount - 1) // 2
    source_of, receiver = lengths[1:1 + 2 * couples:2], lengths[2:2 + 2 * couples:2]
    slack = jnp.minimum(source_of - 1, most - receiver)
    moved = jax.random.randint(jax.random.fold_in(rng, 1), (couples,), 0, 1 << 20) % (slack + 1)
    lengths = lengths.at[1:1 + 2 * couples:2].set(source_of - moved).at[2:2 + 2 * couples:2].set(receiver + moved)
    return lengths[jax.random.permutation(jax.random.fold_in(rng, 2), amount)]


def gaussian(stream_key, extent, deviation, reach, shards=(), kind=jnp.bfloat16):
    values = jax.random.normal(stream_key, extent, jnp.float32) * deviation
    if len(shards) > 0:
        values = level_of(stream_key, extent, shards, -0.22, 0.18) * values
    return jnp.clip(values, min=-reach, max=reach).astype(kind)


def setup_inputs(seed: int = 0) -> dict:
    streams_of = jax.random.split(jax.random.key(seed), 9)
    features = gaussian(streams_of[0], (FIN, NODES), 1.0, 6.0, ((0, 8), (1, 64)))
    order = draw_order(jax.random.fold_in(streams_of[8], 71), 0)
    weight = gaussian(streams_of[2], (FIN, HID), FIN ** -0.5, 0.5, ((1, 8),))
    bias = gaussian(streams_of[3], (HID,), 0.5, 3.0, ((0, 8),))
    tiles = gaussian(streams_of[4], (BLOCKS, K, TILE, TILE), (K * TILE // 2) ** -0.5, 0.09375, ((0, 64),))
    coords = touch_ends(jax.random.randint(streams_of[5], (BLOCKS, K), 0, BLOCKS), jax.random.fold_in(streams_of[5], 1), 0, BLOCKS - 1).astype(jnp.int32)
    counts = ragged(streams_of[6], BLOCKS, BLOCKS * K // 2, K, 2).astype(jnp.int32)
    grad_hidden = gaussian(streams_of[7], (HID, NODES), 1.0, 6.0, ((0, 8), (1, 64)))
    return {"features": features, "order": order, "weight": weight, "bias": bias, "tiles": tiles, "coords": coords, "counts": counts, "grad_hidden": grad_hidden}


def reference(features, order, weight, bias, tiles, coords, counts, grad_hidden):
    reordered = features[:, order]
    slot_live = (jnp.arange(K, dtype=jnp.int32)[None, :] < counts[:, None]).astype(jnp.float32)
    projected = jnp.dot(weight.T, reordered, preferred_element_type=jnp.float32)
    projected_blocks = projected.reshape(HID, BLOCKS, TILE)

    def forward_row(inputs):
        tile_row, coord_row, live_row = inputs
        picked = projected_blocks[:, coord_row, :] * live_row[None, :, None]
        return jnp.einsum('fkc,krc->fr', picked, tile_row.astype(jnp.float32), precision=lax.Precision.HIGHEST)
    summed = lax.map(forward_row, (tiles, coords, slot_live))
    pre_act = jnp.transpose(summed, (1, 0, 2)).reshape(HID, NODES) + bias.astype(jnp.float32)[:, None]
    gate_value = jax.nn.sigmoid(pre_act)
    hidden = (pre_act * gate_value).astype(jnp.bfloat16)
    grad_pre = grad_hidden.astype(jnp.float32) * gate_value * (1.0 + pre_act * (1.0 - gate_value))
    grad_blocks = jnp.transpose(grad_pre.reshape(HID, BLOCKS, TILE), (1, 0, 2))

    def backward_row(carry, inputs):
        tile_row, coord_row, live_row, grad_row = inputs
        contrib = jnp.einsum('fr,krc->kfc', grad_row, tile_row.astype(jnp.float32), precision=lax.Precision.HIGHEST)
        contrib = contrib * live_row[:, None, None]
        carry = carry.at[:, coord_row, :].add(jnp.transpose(contrib, (1, 0, 2)))
        return (carry, None)
    start_sum = jnp.zeros((HID, BLOCKS, TILE), jnp.float32)
    column_grad, _ = lax.scan(backward_row, start_sum, (tiles, coords, slot_live, grad_blocks))
    column_grad = column_grad.reshape(HID, NODES)
    grad_features = jnp.dot(weight.astype(jnp.float32), column_grad, precision=lax.Precision.HIGHEST)
    norm_factor = 1.0 / math.sqrt(NODES)
    grad_weight = jnp.dot(reordered.astype(jnp.float32), column_grad.T, precision=lax.Precision.HIGHEST) * norm_factor
    grad_bias = lax.optimization_barrier(jnp.sum(grad_pre, axis=1)) * norm_factor
    return (hidden, grad_features, grad_weight, grad_bias)
```

```python
import functools
import math

import jax
import jax.numpy as jnp
from jax import lax
from jax.experimental import pallas as pl
from jax.experimental.pallas import tpu as pltpu
from jax.sharding import PartitionSpec as P

INNER = 4
GROUP = 8
F32 = jnp.float32
BF16 = jnp.bfloat16
VMEM = pl.BlockSpec(memory_space=pltpu.VMEM)
SMEM = pl.BlockSpec(memory_space=pltpu.SMEM)


def mm(a, b, ca=1, cb=0):
    return lax.dot_general(a, b, (((ca,), (cb,)), ((), ())), preferred_element_type=F32)


def split2(v):
    high = v.astype(BF16)
    return high, (v - high.astype(F32)).astype(BF16)


def reorder_kernel(order_ref, features_ref, out_ref):
    nodes = features_ref.shape[1]
    half = nodes // 2
    feats = features_ref.shape[0]
    local = jnp.bitwise_and(order_ref[...], nodes - 1)
    source = lax.broadcasted_iota(jnp.int32, (nodes, nodes), 0)
    onehot = (source == local).astype(F32).astype(BF16)
    picked = mm(features_ref[...], onehot).astype(BF16)
    for peer in range(out_ref.shape[0]):
        out_ref[peer, :feats, :] = picked[:, :half]
        out_ref[peer, feats:, :] = picked[:, half:]


def forward_kernel(coords_ref, counts_ref, source_ref, tiles_ref, grad_ref, weight_ref, bias_ref, out_ref):
    blocks, slots, tile, _ = tiles_ref.shape
    feats = source_ref.shape[1]
    units = grad_ref.shape[0]
    peers = out_ref.shape[0]
    parts = []
    for i in range(blocks):
        count = counts_ref[i]

        def body(g, acc, i=i, count=count):
            first = g * GROUP
            left, right = [], []
            for u in range(GROUP):
                slot = first + u
                block = source_ref[coords_ref[i, slot]]
                left.append(jnp.where(slot < count, block, jnp.zeros_like(block)))
                right.append(tiles_ref[i, slot])
            return acc + mm(jnp.concatenate(left, axis=1), jnp.concatenate(right, axis=1), 1, 1)

        groups = lax.div(count + (GROUP - 1), GROUP)
        parts.append(lax.fori_loop(0, groups, body, jnp.zeros((feats, tile), F32)))
    rows = blocks * feats
    high, low = split2(jnp.concatenate(parts, axis=0))
    grad = grad_ref[...]
    base = 2 * rows
    for peer in range(peers):
        out_ref[peer, :rows, :] = high
        out_ref[peer, rows:base, :] = low
        for i in range(blocks):
            out_ref[peer, base + i * units:base + (i + 1) * units, :] = grad[:, i * tile:(i + 1) * tile]
        at = base + blocks * units
        out_ref[peer, at:at + units, :] = weight_ref[...]
        out_ref[peer, at + units:, :] = bias_ref[...]


def backward_kernel(coords_ref, counts_ref, me_ref, message_ref, tiles_ref, hidden_ref, out_ref, silu_ref, grad_ref, term_ref):
    blocks, slots, tile, _ = tiles_ref.shape
    peers = message_ref.shape[0]
    units = hidden_ref.shape[0]
    feats = term_ref.shape[1] // peers
    rows = blocks * feats
    base = 2 * rows
    at = base + blocks * units
    me = me_ref[0]
    chunk = out_ref.shape[1] - (units + 8)

    for part in range(out_ref.shape[0]):
        out_ref[part, :chunk, :] = jnp.zeros((chunk, tile), F32)

    weight = jnp.concatenate([message_ref[p, at:at + units, :] for p in range(peers)], axis=0)
    eye = lax.broadcasted_iota(jnp.int32, (units, tile), 0) == lax.broadcasted_iota(jnp.int32, (units, tile), 1)
    bias = jnp.concatenate(
        [
            jnp.sum(jnp.where(eye, message_ref[p, at + units:, :][:1].astype(F32), 0.0), axis=1, keepdims=True)
            for p in range(peers)
        ],
        axis=0,
    )
    weight_sum = jnp.zeros((units, peers * feats), F32)
    bias_sum = jnp.zeros((8, units), F32)
    ones = jnp.ones((8, tile), BF16)
    mine = pl.ds(pl.multiple_of(me * units, units), units)
    mine_rows = pl.ds(pl.multiple_of(me * feats, feats), feats)
    terms = []
    for i in range(blocks):
        high = jnp.concatenate([message_ref[p, i * feats:(i + 1) * feats, :] for p in range(peers)], axis=0)
        low = jnp.concatenate([message_ref[p, rows + i * feats:rows + (i + 1) * feats, :] for p in range(peers)], axis=0)
        cotangent = jnp.concatenate(
            [message_ref[p, base + i * units:base + (i + 1) * units, :] for p in range(peers)], axis=0
        ).astype(F32)
        pre_act = mm(weight, high) + mm(weight, low) + bias
        gate = 1.0 / (1.0 + jnp.exp(-pre_act))
        silu_ref[...] = pre_act * gate
        hidden_ref[:, i * tile:(i + 1) * tile] = silu_ref[mine, :].astype(BF16)
        grad_pre = cotangent * gate * (1.0 + pre_act * (1.0 - gate))
        grad_ref[...] = grad_pre
        grad_high, grad_low = split2(grad_pre)
        term_ref[i] = mm(weight, grad_high, 0, 0) + mm(weight, grad_low, 0, 0)
        own_high, own_low = split2(grad_ref[mine, :])
        weight_sum = weight_sum + mm(own_high, high, 1, 1) + (mm(own_high, low, 1, 1) + mm(own_low, high, 1, 1))
        bias_sum = bias_sum + mm(ones, own_high, 1, 1) + mm(ones, own_low, 1, 1)
        terms.append(jnp.concatenate(split2(term_ref[i, mine_rows, :]), axis=0))

    bias_wide = jnp.concatenate([bias_sum, jnp.zeros((8, tile - units), F32)], axis=1)
    for part in range(out_ref.shape[0]):
        out_ref[part, chunk:chunk + units, :] = weight_sum
        out_ref[part, chunk + units:, :] = bias_wide

    for i in range(blocks):
        count = counts_ref[i]
        left = terms[i]

        def body(g, carry, i=i, count=count, left=left):
            first = g * GROUP
            product = mm(left, jnp.concatenate([tiles_ref[i, first + u] for u in range(GROUP)], axis=1))
            for u in range(GROUP):
                slot = first + u
                block = coords_ref[i, slot]
                owner = lax.div(block, blocks)
                offset = lax.div(owner, INNER) * rows + lax.rem(block, blocks) * feats
                value = product[:feats, u * tile:(u + 1) * tile] + product[feats:, u * tile:(u + 1) * tile]
                value = jnp.where(slot < count, value, 0.0)
                where = pl.ds(pl.multiple_of(offset, feats), feats)
                part = lax.rem(owner, INNER)
                out_ref[part, where, :] = out_ref[part, where, :] + value
            return carry

        lax.fori_loop(0, lax.div(count + (GROUP - 1), GROUP), body, 0)


def middle_kernel(in_ref, out_ref):
    peers, width, _ = out_ref.shape
    count = in_ref.shape[0]
    extra = (peers * width - in_ref.shape[1]) // (peers - 1)
    rows = width - extra
    shared = functools.reduce(lambda a, b: a + b, [in_ref[s, peers * rows:, :] for s in range(count)])
    for p in range(peers):
        part = functools.reduce(lambda a, b: a + b, [in_ref[s, p * rows:(p + 1) * rows, :] for s in range(count)])
        out_ref[p, :rows, :] = part
        out_ref[p, rows:, :] = shared


def final_kernel(norm_factor, in_ref, grad_ref, weight_ref, bias_ref):
    count = in_ref.shape[0]
    total = functools.reduce(lambda a, b: a + b, [in_ref[s] for s in range(count)])
    feats, nodes = grad_ref.shape
    tile = total.shape[1]
    blocks = nodes // tile
    for i in range(blocks):
        grad_ref[:, i * tile:(i + 1) * tile] = total[i * feats:(i + 1) * feats]
    rows = blocks * feats
    units = weight_ref.shape[0]
    weight_ref[...] = total[rows:rows + units] * norm_factor
    bias_ref[...] = total[rows + units:] * norm_factor


def call(kernel, out_shape, inputs, scalars=0, scratch=(), vmem=40 << 20):
    return pl.pallas_call(
        kernel,
        out_shape=out_shape,
        in_specs=[SMEM] * scalars + [VMEM] * (len(inputs) - scalars),
        out_specs=jax.tree.map(lambda _: VMEM, out_shape),
        scratch_shapes=scratch,
        compiler_params=pltpu.CompilerParams(vmem_limit_bytes=vmem),
    )(*inputs)


def per_device(row_size, col_size, features, order, weight, bias, tiles, coords, counts, grad_hidden):
    feats, nodes = features.shape
    units = weight.shape[1]
    blocks, slots, tile, _ = tiles.shape
    rows = blocks * feats
    outer = row_size // INNER
    norm_factor = 1.0 / math.sqrt(nodes * row_size)
    inner_groups = [[q * INNER + x for x in range(INNER)] for q in range(outer)]
    outer_groups = [[q * INNER + x for q in range(outer)] for x in range(INNER)]

    spread = call(
        reorder_kernel, jax.ShapeDtypeStruct((row_size, rows, tile), BF16), (order.reshape(1, nodes), features)
    )
    everywhere = lax.all_to_all(spread, "row", 0, 0, tiled=True)
    source = everywhere.reshape(row_size * blocks, feats, tile)
    bias_rows = jnp.pad(bias.reshape(1, units), ((0, 15), (0, tile - units)))
    height = 2 * rows + blocks * units + units + 16
    message = call(
        forward_kernel,
        jax.ShapeDtypeStruct((col_size, height, tile), BF16),
        (coords, counts, source, tiles, grad_hidden, weight.T, bias_rows),
        scalars=2,
    )
    message = lax.all_to_all(message, "col", 0, 0, tiled=True)
    me = lax.axis_index("col").reshape(1)
    chunk = outer * rows
    hidden, partial = call(
        backward_kernel,
        (
            jax.ShapeDtypeStruct((units, nodes), BF16),
            jax.ShapeDtypeStruct((INNER, chunk + units + 8, tile), F32),
        ),
        (coords, counts, me, message, tiles),
        scalars=3,
        scratch=[
            pltpu.VMEM((units * col_size, tile), F32),
            pltpu.VMEM((units * col_size, tile), F32),
            pltpu.VMEM((blocks, feats * col_size, tile), F32),
        ],
    )
    partial = lax.all_to_all(partial, "row", 0, 0, tiled=True, axis_index_groups=inner_groups)
    second = call(middle_kernel, jax.ShapeDtypeStruct((outer, rows + units + 8, tile), F32), (partial,))
    second = lax.all_to_all(second, "row", 0, 0, tiled=True, axis_index_groups=outer_groups)
    grad_features, grad_weight, grad_bias = call(
        functools.partial(final_kernel, norm_factor),
        (
            jax.ShapeDtypeStruct((feats, nodes), F32),
            jax.ShapeDtypeStruct((units, tile), F32),
            jax.ShapeDtypeStruct((8, tile), F32),
        ),
        (second,),
    )
    return hidden, grad_features, grad_weight.T, grad_bias[0, :units]


def solution(mesh):
    in_specs = (
        P("col", "row"),
        P("row"),
        P(None, "col"),
        P("col"),
        P("row", None, None, None),
        P("row", None),
        P("row"),
        P("col", "row"),
    )
    out_specs = (P("col", "row"), P("col", "row"), P(None, "col"), P("col"))
    body = functools.partial(per_device, mesh.shape["row"], mesh.shape["col"])
    return jax.shard_map(body, mesh=mesh, in_specs=in_specs, out_specs=out_specs, check_vma=False)
```

```python
import functools
import math

import jax
import jax.numpy as jnp
from jax import lax
from jax.experimental import pallas as pl
from jax.experimental.pallas import tpu as pltpu
from jax.sharding import PartitionSpec as P

INNER = 4
GROUP = 8
TILE_VMEM = 51 << 20
SMALL_VMEM = 60 << 20
F32 = jnp.float32
BF16 = jnp.bfloat16
VMEM = pl.BlockSpec(memory_space=pltpu.VMEM)
SPECS = {"v": VMEM, "s": pl.BlockSpec(memory_space=pltpu.SMEM), "h": pl.BlockSpec(memory_space=pltpu.HBM)}


def mm(a, b, ca=1, cb=0):
    return lax.dot_general(a, b, (((ca,), (cb,)), ((), ())), preferred_element_type=F32)


def split2(v):
    high = v.astype(BF16)
    return high, (v - high.astype(F32)).astype(BF16)


def reorder_kernel(order_hbm, features_hbm, grad_hbm, weight_hbm, bias_hbm, out_ref, static_ref, order_ref, features_ref, grad_ref, weight_ref, bias_ref, sems):
    pairs = (
        (order_hbm, order_ref),
        (features_hbm, features_ref),
        (grad_hbm, grad_ref),
        (weight_hbm, weight_ref),
        (bias_hbm, bias_ref),
    )
    copies = [pltpu.make_async_copy(src, dst, sems.at[n]) for n, (src, dst) in enumerate(pairs)]
    for copy in copies:
        copy.start()
    feats, nodes = features_ref.shape
    tile = out_ref.shape[2]
    blocks = nodes // tile
    copies[0].wait()
    local = jnp.bitwise_and(order_ref[...], nodes - 1)
    source = lax.broadcasted_iota(jnp.int32, (nodes, nodes), 0)
    onehot = (source == local).astype(F32).astype(BF16)
    copies[1].wait()
    picked = mm(features_ref[...], onehot).astype(BF16)
    for peer in range(out_ref.shape[0]):
        for i in range(blocks):
            out_ref[peer, i * feats:(i + 1) * feats, :] = picked[:, i * tile:(i + 1) * tile]
    for copy in copies[2:]:
        copy.wait()
    units = grad_ref.shape[0]
    grad = grad_ref[...]
    bias = jnp.concatenate([bias_ref[...].astype(F32), jnp.zeros((1, tile - units), F32)], axis=1)
    bias = jnp.broadcast_to(bias, (16, tile)).astype(BF16)
    for i in range(blocks):
        static_ref[i * units:(i + 1) * units, :] = grad[:, i * tile:(i + 1) * tile]
    at = blocks * units
    static_ref[at:at + units, :] = weight_ref[...]
    static_ref[at + units:, :] = bias


def tile_copy(tiles_hbm, tiles_ref, sems, i, g):
    where = pl.ds(g * GROUP, GROUP)
    return pltpu.make_async_copy(tiles_hbm.at[i, where], tiles_ref.at[i, where], sems.at[i, g])


def start_tiles(tiles_hbm, tiles_ref, sems):
    for i in range(tiles_ref.shape[0]):

        def body(g, carry, i=i):
            tile_copy(tiles_hbm, tiles_ref, sems, i, g).start()
            return carry

        lax.fori_loop(0, sems.shape[1], body, 0)


def wait_rest(tiles_hbm, tiles_ref, sems, i, first):
    def body(g, carry):
        tile_copy(tiles_hbm, tiles_ref, sems, i, g).wait()
        return carry

    lax.fori_loop(first, sems.shape[1], body, 0)


def forward_kernel(coords_ref, counts_ref, source_ref, tiles_hbm, out_ref, tiles_ref, sems):
    blocks, slots, tile, _ = tiles_ref.shape
    feats = source_ref.shape[1]
    peers = out_ref.shape[0]
    start_tiles(tiles_hbm, tiles_ref, sems)
    parts = []
    for i in range(blocks):
        count = counts_ref[i]
        groups = lax.div(count + (GROUP - 1), GROUP)

        def body(g, acc, i=i, count=count):
            first = g * GROUP
            left = []
            for u in range(GROUP):
                block = source_ref[coords_ref[i, first + u]]
                left.append(jnp.where(first + u < count, block, jnp.zeros_like(block)))
            left = jnp.concatenate(left, axis=1)
            tile_copy(tiles_hbm, tiles_ref, sems, i, g).wait()
            right = jnp.concatenate([tiles_ref[i, first + u] for u in range(GROUP)], axis=1)
            return acc + mm(left, right, 1, 1)

        parts.append(lax.fori_loop(0, groups, body, jnp.zeros((feats, tile), F32)))
        wait_rest(tiles_hbm, tiles_ref, sems, i, groups)
    rows = blocks * feats
    high, low = split2(jnp.concatenate(parts, axis=0))
    for peer in range(peers):
        out_ref[peer, :rows, :] = high
        out_ref[peer, rows:, :] = low


def backward_kernel(
    coords_ref, counts_ref, message_ref, static_ref, tiles_hbm, hidden_ref, out_ref, tiles_ref, silu_ref, grad_ref, term_ref, sems
):
    blocks, slots, tile, _ = tiles_ref.shape
    peers = message_ref.shape[0]
    units = hidden_ref.shape[0]
    feats = term_ref.shape[1] // peers
    rows = blocks * feats
    at = blocks * units
    me = lax.axis_index("col")
    chunk = out_ref.shape[1] - (units + 8)
    start_tiles(tiles_hbm, tiles_ref, sems)

    for part in range(out_ref.shape[0]):
        out_ref[part, :chunk, :] = jnp.zeros((chunk, tile), F32)

    weight = jnp.concatenate([static_ref[p, at:at + units, :] for p in range(peers)], axis=0)
    eye = lax.broadcasted_iota(jnp.int32, (units, tile), 0) == lax.broadcasted_iota(jnp.int32, (units, tile), 1)
    bias = jnp.concatenate(
        [
            jnp.sum(jnp.where(eye, static_ref[p, at + units:, :][:1].astype(F32), 0.0), axis=1, keepdims=True)
            for p in range(peers)
        ],
        axis=0,
    )
    weight_sum = jnp.zeros((units, peers * feats), F32)
    bias_sum = jnp.zeros((8, units), F32)
    ones = jnp.ones((8, tile), BF16)
    mine = pl.ds(pl.multiple_of(me * units, units), units)
    mine_rows = pl.ds(pl.multiple_of(me * feats, feats), feats)
    terms = []
    for i in range(blocks):
        high = jnp.concatenate([message_ref[p, i * feats:(i + 1) * feats, :] for p in range(peers)], axis=0)
        low = jnp.concatenate([message_ref[p, rows + i * feats:rows + (i + 1) * feats, :] for p in range(peers)], axis=0)
        cotangent = jnp.concatenate([static_ref[p, i * units:(i + 1) * units, :] for p in range(peers)], axis=0).astype(F32)
        pre_act = mm(weight, high) + mm(weight, low) + bias
        gate = 1.0 / (1.0 + jnp.exp(-pre_act))
        silu_ref[...] = pre_act * gate
        hidden_ref[:, i * tile:(i + 1) * tile] = silu_ref[mine, :].astype(BF16)
        grad_pre = cotangent * gate * (1.0 + pre_act * (1.0 - gate))
        grad_ref[...] = grad_pre
        grad_high, grad_low = split2(grad_pre)
        term_ref[i] = mm(weight, grad_high, 0, 0) + mm(weight, grad_low, 0, 0)
        own_high, own_low = split2(grad_ref[mine, :])
        weight_sum = weight_sum + mm(own_high, high, 1, 1) + (mm(own_high, low, 1, 1) + mm(own_low, high, 1, 1))
        bias_sum = bias_sum + mm(ones, own_high, 1, 1) + mm(ones, own_low, 1, 1)
        terms.append(jnp.concatenate(split2(term_ref[i, mine_rows, :]), axis=0))

    bias_wide = jnp.concatenate([bias_sum, jnp.zeros((8, tile - units), F32)], axis=1)
    for part in range(out_ref.shape[0]):
        out_ref[part, chunk:chunk + units, :] = weight_sum
        out_ref[part, chunk + units:, :] = bias_wide

    for i in range(blocks):
        count = counts_ref[i]
        left = terms[i]
        groups = lax.div(count + (GROUP - 1), GROUP)

        def body(g, carry, i=i, count=count, left=left):
            first = g * GROUP
            tile_copy(tiles_hbm, tiles_ref, sems, i, g).wait()
            product = mm(left, jnp.concatenate([tiles_ref[i, first + u] for u in range(GROUP)], axis=1))
            for u in range(GROUP):
                slot = first + u
                block = coords_ref[i, slot]
                owner = lax.div(block, blocks)
                offset = lax.div(owner, INNER) * rows + lax.rem(block, blocks) * feats
                value = product[:feats, u * tile:(u + 1) * tile] + product[feats:, u * tile:(u + 1) * tile]
                value = jnp.where(slot < count, value, 0.0)
                where = pl.ds(pl.multiple_of(offset, feats), feats)
                part = lax.rem(owner, INNER)
                out_ref[part, where, :] = out_ref[part, where, :] + value
            return carry

        lax.fori_loop(0, groups, body, 0)
        wait_rest(tiles_hbm, tiles_ref, sems, i, groups)


def middle_kernel(in_ref, out_ref):
    peers, width, _ = out_ref.shape
    count = in_ref.shape[0]
    extra = (peers * width - in_ref.shape[1]) // (peers - 1)
    rows = width - extra
    shared = functools.reduce(lambda a, b: a + b, [in_ref[s, peers * rows:, :] for s in range(count)])
    for p in range(peers):
        part = functools.reduce(lambda a, b: a + b, [in_ref[s, p * rows:(p + 1) * rows, :] for s in range(count)])
        out_ref[p, :rows, :] = part
        out_ref[p, rows:, :] = shared


def final_kernel(norm_factor, in_ref, grad_ref, weight_ref, bias_ref):
    count = in_ref.shape[0]
    total = functools.reduce(lambda a, b: a + b, [in_ref[s] for s in range(count)])
    feats, nodes = grad_ref.shape
    tile = total.shape[1]
    blocks = nodes // tile
    for i in range(blocks):
        grad_ref[:, i * tile:(i + 1) * tile] = total[i * feats:(i + 1) * feats]
    rows = blocks * feats
    units = weight_ref.shape[0]
    weight_ref[...] = total[rows:rows + units] * norm_factor
    bias_ref[...] = total[rows + units:rows + units + 1, :units] * norm_factor


def call(kernel, out_shape, inputs, specs, scratch=(), vmem=40 << 20):
    return pl.pallas_call(
        kernel,
        out_shape=out_shape,
        in_specs=[SPECS[c] for c in specs],
        out_specs=jax.tree.map(lambda _: VMEM, out_shape),
        scratch_shapes=scratch,
        compiler_params=pltpu.CompilerParams(vmem_limit_bytes=vmem),
    )(*inputs)


def per_device(row_size, col_size, features, order, weight, bias, tiles, coords, counts, grad_hidden):
    feats, nodes = features.shape
    units = weight.shape[1]
    blocks, slots, tile, _ = tiles.shape
    rows = blocks * feats
    outer = row_size // INNER
    norm_factor = 1.0 / math.sqrt(nodes * row_size)
    inner_groups = [[q * INNER + x for x in range(INNER)] for q in range(outer)]
    outer_groups = [[q * INNER + x for q in range(outer)] for x in range(INNER)]
    tile_scratch = pltpu.VMEM(tiles.shape, BF16)
    tile_sems = pltpu.SemaphoreType.DMA((blocks, slots // GROUP))

    spread, static = call(
        reorder_kernel,
        (
            jax.ShapeDtypeStruct((row_size, rows, tile), BF16),
            jax.ShapeDtypeStruct((blocks * units + units + 16, tile), BF16),
        ),
        (order.reshape(1, nodes), features, grad_hidden, weight.T, bias.reshape(1, units)),
        "hhhhh",
        scratch=[
            pltpu.VMEM((1, nodes), jnp.int32),
            pltpu.VMEM(features.shape, BF16),
            pltpu.VMEM(grad_hidden.shape, BF16),
            pltpu.VMEM((units, tile), BF16),
            pltpu.VMEM((1, units), BF16),
            pltpu.SemaphoreType.DMA((5,)),
        ],
        vmem=SMALL_VMEM,
    )
    everywhere = lax.all_to_all(spread, "row", 0, 0, tiled=True)
    static = lax.all_gather(static, "col", axis=0)
    everywhere, static = lax.optimization_barrier((everywhere, static))
    source = everywhere.reshape(row_size * blocks, feats, tile)
    message = call(
        forward_kernel,
        jax.ShapeDtypeStruct((col_size, 2 * rows, tile), BF16),
        (coords, counts, source, tiles),
        "ssvh",
        scratch=[tile_scratch, tile_sems],
        vmem=TILE_VMEM,
    )
    message = lax.all_to_all(message, "col", 0, 0, tiled=True)
    chunk = outer * rows
    hidden, partial = call(
        backward_kernel,
        (
            jax.ShapeDtypeStruct((units, nodes), BF16),
            jax.ShapeDtypeStruct((INNER, chunk + units + 8, tile), F32),
        ),
        (coords, counts, message, static, tiles),
        "ssvvh",
        scratch=[
            tile_scratch,
            pltpu.VMEM((units * col_size, tile), F32),
            pltpu.VMEM((units * col_size, tile), F32),
            pltpu.VMEM((blocks, feats * col_size, tile), F32),
            tile_sems,
        ],
        vmem=TILE_VMEM,
    )
    partial = lax.all_to_all(partial, "row", 0, 0, tiled=True, axis_index_groups=inner_groups)
    second = call(middle_kernel, jax.ShapeDtypeStruct((outer, rows + units + 8, tile), F32), (partial,), "v")
    second = lax.all_to_all(second, "row", 0, 0, tiled=True, axis_index_groups=outer_groups)
    grad_features, grad_weight, grad_bias = call(
        functools.partial(final_kernel, norm_factor),
        (
            jax.ShapeDtypeStruct((feats, nodes), F32),
            jax.ShapeDtypeStruct((units, tile), F32),
            jax.ShapeDtypeStruct((1, units), F32),
        ),
        (second,),
        "v",
    )
    return hidden, grad_features, grad_weight.T, grad_bias.reshape(units)


def solution(mesh):
    in_specs = (
        P("col", "row"),
        P("row"),
        P(None, "col"),
        P("col"),
        P("row", None, None, None),
        P("row", None),
        P("row"),
        P("col", "row"),
    )
    out_specs = (P("col", "row"), P("col", "row"), P(None, "col"), P("col"))
    body = functools.partial(per_device, mesh.shape["row"], mesh.shape["col"])
    return jax.shard_map(body, mesh=mesh, in_specs=in_specs, out_specs=out_specs, check_vma=False)
```

```python
import functools
import math

import jax
import jax.numpy as jnp
from jax import lax
from jax.experimental import pallas as pl
from jax.experimental.pallas import tpu as pltpu
from jax.sharding import PartitionSpec as P

INNER = 4
GROUP = 8
SMALL_VMEM = 60 << 20
TILE_VMEM = 51 << 20
STAGE_VMEM = 51 << 20
GATHER_BYTES = 1 << 20
F32 = jnp.float32
BF16 = jnp.bfloat16
VMEM = pl.BlockSpec(memory_space=pltpu.VMEM)
SPECS = {"v": VMEM, "s": pl.BlockSpec(memory_space=pltpu.SMEM), "h": pl.BlockSpec(memory_space=pltpu.HBM)}


def mm(a, b, ca=1, cb=0):
    return lax.dot_general(a, b, (((ca,), (cb,)), ((), ())), preferred_element_type=F32)


def split2(v):
    high = v.astype(BF16)
    return high, (v - high.astype(F32)).astype(BF16)


def reorder_kernel(order_hbm, features_hbm, grad_hbm, weight_hbm, bias_hbm, out_ref, static_ref, order_ref, features_ref, grad_ref, weight_ref, bias_ref, sems):
    pairs = (
        (order_hbm, order_ref),
        (features_hbm, features_ref),
        (grad_hbm, grad_ref),
        (weight_hbm, weight_ref),
        (bias_hbm, bias_ref),
    )
    copies = [pltpu.make_async_copy(src, dst, sems.at[n]) for n, (src, dst) in enumerate(pairs)]
    for copy in copies:
        copy.start()
    feats, nodes = features_ref.shape
    tile = out_ref.shape[2]
    blocks = nodes // tile
    copies[0].wait()
    local = jnp.bitwise_and(order_ref[...], nodes - 1)
    source = lax.broadcasted_iota(jnp.int32, (nodes, nodes), 0)
    onehot = (source == local).astype(F32).astype(BF16)
    copies[1].wait()
    picked = mm(features_ref[...], onehot).astype(BF16)
    for peer in range(out_ref.shape[0]):
        for i in range(blocks):
            out_ref[peer, i * feats:(i + 1) * feats, :] = picked[:, i * tile:(i + 1) * tile]
    for copy in copies[2:]:
        copy.wait()
    units = grad_ref.shape[0]
    grad = grad_ref[...]
    bias = jnp.concatenate([bias_ref[...].astype(F32), jnp.zeros((1, tile - units), F32)], axis=1)
    bias = jnp.broadcast_to(bias, (16, tile)).astype(BF16)
    for i in range(blocks):
        static_ref[i * units:(i + 1) * units, :] = grad[:, i * tile:(i + 1) * tile]
    at = blocks * units
    static_ref[at:at + units, :] = weight_ref[...]
    static_ref[at + units:at + units + 16, :] = bias
    rest = static_ref.shape[0] - (at + units + 16)
    static_ref[at + units + 16:, :] = jnp.zeros((rest, tile), BF16)


def stage_kernel(tiles_hbm, out_ref, sem):
    copy = pltpu.make_async_copy(tiles_hbm.at[0], out_ref, sem)
    copy.start()
    copy.wait()


def forward_kernel(coords_ref, counts_ref, source_ref, staged_ref, tiles_hbm, out_ref, later_ref, sem):
    blocks, slots, tile, _ = tiles_hbm.shape
    copy = pltpu.make_async_copy(tiles_hbm.at[pl.ds(1, blocks - 1)], later_ref, sem)
    copy.start()
    feats = source_ref.shape[1]
    peers = out_ref.shape[0]
    parts = []
    for i in range(blocks):
        tiles_ref = staged_ref if i == 0 else later_ref.at[i - 1]
        if i == 1:
            copy.wait()
        count = counts_ref[i]
        groups = lax.div(count + (GROUP - 1), GROUP)

        def body(g, acc, i=i, count=count, tiles_ref=tiles_ref):
            first = g * GROUP
            left = []
            for u in range(GROUP):
                block = source_ref[coords_ref[i, first + u]]
                left.append(jnp.where(first + u < count, block, jnp.zeros_like(block)))
            left = jnp.concatenate(left, axis=1)
            right = jnp.concatenate([tiles_ref[first + u] for u in range(GROUP)], axis=1)
            return acc + mm(left, right, 1, 1)

        parts.append(lax.fori_loop(0, groups, body, jnp.zeros((feats, tile), F32)))
    rows = blocks * feats
    high, low = split2(jnp.concatenate(parts, axis=0))
    for peer in range(peers):
        out_ref[peer, :rows, :] = high
        out_ref[peer, rows:, :] = low


def backward_kernel(
    coords_ref, counts_ref, message_ref, static_hbm, tiles_hbm, hidden_ref, out_ref, all_ref, static_ref, silu_ref, grad_ref, term_ref, tile_sems, sem
):
    blocks, slots, tile, _ = tiles_hbm.shape
    tile_copies = [pltpu.make_async_copy(tiles_hbm.at[i], all_ref.at[i], tile_sems.at[i]) for i in range(blocks)]
    for tile_copy in tile_copies:
        tile_copy.start()
    copy = pltpu.make_async_copy(static_hbm.at[:, pl.ds(0, static_ref.shape[1])], static_ref, sem)
    copy.start()
    peers = message_ref.shape[0]
    units = hidden_ref.shape[0]
    feats = term_ref.shape[1] // peers
    rows = blocks * feats
    at = blocks * units
    me = lax.axis_index("col")
    chunk = out_ref.shape[1] - (units + 8)

    for part in range(out_ref.shape[0]):
        out_ref[part, :chunk, :] = jnp.zeros((chunk, tile), F32)
    copy.wait()

    weight = jnp.concatenate([static_ref[p, at:at + units, :] for p in range(peers)], axis=0)
    eye = lax.broadcasted_iota(jnp.int32, (units, tile), 0) == lax.broadcasted_iota(jnp.int32, (units, tile), 1)
    bias = jnp.concatenate(
        [
            jnp.sum(jnp.where(eye, static_ref[p, at + units:, :][:1].astype(F32), 0.0), axis=1, keepdims=True)
            for p in range(peers)
        ],
        axis=0,
    )
    weight_sum = jnp.zeros((units, peers * feats), F32)
    bias_sum = jnp.zeros((8, units), F32)
    ones = jnp.ones((8, tile), BF16)
    mine = pl.ds(pl.multiple_of(me * units, units), units)
    mine_rows = pl.ds(pl.multiple_of(me * feats, feats), feats)
    terms = []
    for i in range(blocks):
        high = jnp.concatenate([message_ref[p, i * feats:(i + 1) * feats, :] for p in range(peers)], axis=0)
        low = jnp.concatenate([message_ref[p, rows + i * feats:rows + (i + 1) * feats, :] for p in range(peers)], axis=0)
        cotangent = jnp.concatenate([static_ref[p, i * units:(i + 1) * units, :] for p in range(peers)], axis=0).astype(F32)
        pre_act = mm(weight, high) + mm(weight, low) + bias
        gate = 1.0 / (1.0 + jnp.exp(-pre_act))
        silu_ref[...] = pre_act * gate
        hidden_ref[:, i * tile:(i + 1) * tile] = silu_ref[mine, :].astype(BF16)
        grad_pre = cotangent * gate * (1.0 + pre_act * (1.0 - gate))
        grad_ref[...] = grad_pre
        grad_high, grad_low = split2(grad_pre)
        term_ref[i] = mm(weight, grad_high, 0, 0) + mm(weight, grad_low, 0, 0)
        own_high, own_low = split2(grad_ref[mine, :])
        weight_sum = weight_sum + mm(own_high, high, 1, 1) + (mm(own_high, low, 1, 1) + mm(own_low, high, 1, 1))
        bias_sum = bias_sum + mm(ones, own_high, 1, 1) + mm(ones, own_low, 1, 1)
        terms.append(jnp.concatenate(split2(term_ref[i, mine_rows, :]), axis=0))

    bias_wide = jnp.concatenate([bias_sum, jnp.zeros((8, tile - units), F32)], axis=1)
    for part in range(out_ref.shape[0]):
        out_ref[part, chunk:chunk + units, :] = weight_sum
        out_ref[part, chunk + units:, :] = bias_wide

    for i in range(blocks):
        tiles_ref = all_ref.at[i]
        tile_copies[i].wait()
        count = counts_ref[i]
        left = terms[i]
        groups = lax.div(count + (GROUP - 1), GROUP)

        def body(g, carry, i=i, count=count, left=left, tiles_ref=tiles_ref):
            first = g * GROUP
            product = mm(left, jnp.concatenate([tiles_ref[first + u] for u in range(GROUP)], axis=1))
            for u in range(GROUP):
                slot = first + u
                block = coords_ref[i, slot]
                owner = lax.div(block, blocks)
                offset = lax.div(owner, INNER) * rows + lax.rem(block, blocks) * feats
                value = product[:feats, u * tile:(u + 1) * tile] + product[feats:, u * tile:(u + 1) * tile]
                value = jnp.where(slot < count, value, 0.0)
                where = pl.ds(pl.multiple_of(offset, feats), feats)
                part = lax.rem(owner, INNER)
                out_ref[part, where, :] = out_ref[part, where, :] + value
            return carry

        lax.fori_loop(0, groups, body, 0)


def middle_kernel(in_ref, out_ref):
    peers, width, _ = out_ref.shape
    count = in_ref.shape[0]
    extra = (peers * width - in_ref.shape[1]) // (peers - 1)
    rows = width - extra
    shared = functools.reduce(lambda a, b: a + b, [in_ref[s, peers * rows:, :] for s in range(count)])
    for p in range(peers):
        part = functools.reduce(lambda a, b: a + b, [in_ref[s, p * rows:(p + 1) * rows, :] for s in range(count)])
        out_ref[p, :rows, :] = part
        out_ref[p, rows:, :] = shared


def final_kernel(norm_factor, in_ref, grad_ref, weight_ref, bias_ref):
    count = in_ref.shape[0]
    total = functools.reduce(lambda a, b: a + b, [in_ref[s] for s in range(count)])
    feats, nodes = grad_ref.shape
    tile = total.shape[1]
    blocks = nodes // tile
    for i in range(blocks):
        grad_ref[:, i * tile:(i + 1) * tile] = total[i * feats:(i + 1) * feats]
    rows = blocks * feats
    units = weight_ref.shape[0]
    weight_ref[...] = total[rows:rows + units] * norm_factor
    bias_ref[...] = total[rows + units:rows + units + 1, :units] * norm_factor


def call(kernel, out_shape, inputs, specs, scratch=(), vmem=40 << 20, cost=None):
    return pl.pallas_call(
        kernel,
        out_shape=out_shape,
        in_specs=[SPECS[c] for c in specs],
        out_specs=jax.tree.map(lambda _: VMEM, out_shape),
        scratch_shapes=scratch,
        cost_estimate=cost,
        compiler_params=pltpu.CompilerParams(vmem_limit_bytes=vmem),
    )(*inputs)


def per_device(row_size, col_size, features, order, weight, bias, tiles, coords, counts, grad_hidden):
    feats, nodes = features.shape
    units = weight.shape[1]
    blocks, slots, tile, _ = tiles.shape
    rows = blocks * feats
    outer = row_size // INNER
    norm_factor = 1.0 / math.sqrt(nodes * row_size)
    inner_groups = [[q * INNER + x for x in range(INNER)] for q in range(outer)]
    outer_groups = [[q * INNER + x for q in range(outer)] for x in range(INNER)]
    static_rows = blocks * units + units + 16
    padded_rows = max(static_rows, GATHER_BYTES // (2 * tile * col_size))

    spread, static = call(
        reorder_kernel,
        (
            jax.ShapeDtypeStruct((row_size, rows, tile), BF16),
            jax.ShapeDtypeStruct((padded_rows, tile), BF16),
        ),
        (order.reshape(1, nodes), features, grad_hidden, weight.T, bias.reshape(1, units)),
        "hhhhh",
        scratch=[
            pltpu.VMEM((1, nodes), jnp.int32),
            pltpu.VMEM(features.shape, BF16),
            pltpu.VMEM(grad_hidden.shape, BF16),
            pltpu.VMEM((units, tile), BF16),
            pltpu.VMEM((1, units), BF16),
            pltpu.SemaphoreType.DMA((5,)),
        ],
        vmem=SMALL_VMEM,
    )
    everywhere = lax.all_to_all(spread, "row", 0, 0, tiled=True)
    static = lax.all_gather(static, "col", axis=0)
    staged = call(
        stage_kernel,
        jax.ShapeDtypeStruct(tiles.shape[1:], BF16),
        (tiles,),
        "h",
        scratch=[pltpu.SemaphoreType.DMA],
        vmem=STAGE_VMEM,
        cost=pl.CostEstimate(flops=0, transcendentals=0, bytes_accessed=4 * tiles.size // blocks),
    )
    source = everywhere.reshape(row_size * blocks, feats, tile)
    message = call(
        forward_kernel,
        jax.ShapeDtypeStruct((col_size, 2 * rows, tile), BF16),
        (coords, counts, source, staged, tiles),
        "ssvvh",
        scratch=[pltpu.VMEM((blocks - 1,) + tiles.shape[1:], BF16), pltpu.SemaphoreType.DMA],
        vmem=TILE_VMEM,
    )
    message = lax.all_to_all(message, "col", 0, 0, tiled=True)
    chunk = outer * rows
    hidden, partial = call(
        backward_kernel,
        (
            jax.ShapeDtypeStruct((units, nodes), BF16),
            jax.ShapeDtypeStruct((INNER, chunk + units + 8, tile), F32),
        ),
        (coords, counts, message, static, tiles),
        "ssvhh",
        scratch=[
            pltpu.VMEM(tiles.shape, BF16),
            pltpu.VMEM((col_size, static_rows, tile), BF16),
            pltpu.VMEM((units * col_size, tile), F32),
            pltpu.VMEM((units * col_size, tile), F32),
            pltpu.VMEM((blocks, feats * col_size, tile), F32),
            pltpu.SemaphoreType.DMA((blocks,)),
            pltpu.SemaphoreType.DMA,
        ],
        vmem=TILE_VMEM,
    )
    partial = lax.all_to_all(partial, "row", 0, 0, tiled=True, axis_index_groups=inner_groups)
    second = call(middle_kernel, jax.ShapeDtypeStruct((outer, rows + units + 8, tile), F32), (partial,), "v")
    second = lax.all_to_all(second, "row", 0, 0, tiled=True, axis_index_groups=outer_groups)
    grad_features, grad_weight, grad_bias = call(
        functools.partial(final_kernel, norm_factor),
        (
            jax.ShapeDtypeStruct((feats, nodes), F32),
            jax.ShapeDtypeStruct((units, tile), F32),
            jax.ShapeDtypeStruct((1, units), F32),
        ),
        (second,),
        "v",
    )
    return hidden, grad_features, grad_weight.T, grad_bias.reshape(units)


def solution(mesh):
    in_specs = (
        P("col", "row"),
        P("row"),
        P(None, "col"),
        P("col"),
        P("row", None, None, None),
        P("row", None),
        P("row"),
        P("col", "row"),
    )
    out_specs = (P("col", "row"), P("col", "row"), P(None, "col"), P("col"))
    body = functools.partial(per_device, mesh.shape["row"], mesh.shape["col"])
    return jax.shard_map(body, mesh=mesh, in_specs=in_specs, out_specs=out_specs, check_vma=False)
```

```python
import functools
import math

import jax
import jax.numpy as jnp
from jax import lax
from jax.experimental import pallas as pl
from jax.experimental.pallas import tpu as pltpu
from jax.sharding import PartitionSpec as P

INNER = 4
GROUP = 8
SMALL_VMEM = 60 << 20
TILE_VMEM = 51 << 20
F32 = jnp.float32
BF16 = jnp.bfloat16
VMEM = pl.BlockSpec(memory_space=pltpu.VMEM)
SPECS = {"v": VMEM, "s": pl.BlockSpec(memory_space=pltpu.SMEM), "h": pl.BlockSpec(memory_space=pltpu.HBM)}


def mm(a, b, ca=1, cb=0):
    return lax.dot_general(a, b, (((ca,), (cb,)), ((), ())), preferred_element_type=F32)


def split2(v):
    high = v.astype(BF16)
    return high, (v - high.astype(F32)).astype(BF16)


def reorder_kernel(order_hbm, features_hbm, out_ref, order_ref, features_ref, sems):
    pairs = ((order_hbm, order_ref), (features_hbm, features_ref))
    copies = [pltpu.make_async_copy(src, dst, sems.at[n]) for n, (src, dst) in enumerate(pairs)]
    for copy in copies:
        copy.start()
    feats, nodes = features_ref.shape
    tile = out_ref.shape[2]
    blocks = nodes // tile
    copies[0].wait()
    local = jnp.bitwise_and(order_ref[...], nodes - 1)
    source = lax.broadcasted_iota(jnp.int32, (nodes, nodes), 0)
    onehot = (source == local).astype(F32).astype(BF16)
    copies[1].wait()
    picked = mm(features_ref[...], onehot).astype(BF16)
    for peer in range(out_ref.shape[0]):
        for i in range(blocks):
            out_ref[peer, i * feats:(i + 1) * feats, :] = picked[:, i * tile:(i + 1) * tile]


def forward_kernel(coords_ref, counts_ref, source_ref, weight_ref, bias_ref, staged_ref, tiles_hbm, out_ref, later_ref, sem):
    blocks, slots, tile, _ = tiles_hbm.shape
    copy = pltpu.make_async_copy(tiles_hbm.at[pl.ds(1, blocks - 1)], later_ref, sem)
    copy.start()
    feats = source_ref.shape[1]
    peers = out_ref.shape[0]
    parts = []
    for i in range(blocks):
        tiles_ref = staged_ref.at[0] if i == 0 else later_ref.at[i - 1]
        if i == 1:
            copy.wait()
        count = counts_ref[i]
        groups = lax.div(count + (GROUP - 1), GROUP)

        def body(g, acc, i=i, count=count, tiles_ref=tiles_ref):
            first = g * GROUP
            left = []
            for u in range(GROUP):
                block = source_ref[coords_ref[i, first + u]]
                left.append(jnp.where(first + u < count, block, jnp.zeros_like(block)))
            left = jnp.concatenate(left, axis=1)
            right = jnp.concatenate([tiles_ref[first + u] for u in range(GROUP)], axis=1)
            return acc + mm(left, right, 1, 1)

        parts.append(lax.fori_loop(0, groups, body, jnp.zeros((feats, tile), F32)))
    rows = blocks * feats
    high, low = split2(jnp.concatenate(parts, axis=0))
    units = weight_ref.shape[0]
    bias = jnp.concatenate([bias_ref[...].astype(F32), jnp.zeros((1, tile - units), F32)], axis=1)
    bias = jnp.broadcast_to(bias, (16, tile)).astype(BF16)
    for peer in range(peers):
        out_ref[peer, :rows, :] = high
        out_ref[peer, rows:2 * rows, :] = low
        out_ref[peer, 2 * rows:2 * rows + units, :] = weight_ref[...]
        out_ref[peer, 2 * rows + units:, :] = bias


def backward_kernel(
    coords_ref, counts_ref, message_ref, cotangent_ref, tiles_hbm, hidden_ref, out_ref, all_ref, silu_ref, grad_ref, term_ref, tile_sems
):
    blocks, slots, tile, _ = tiles_hbm.shape
    tile_copies = [pltpu.make_async_copy(tiles_hbm.at[i], all_ref.at[i], tile_sems.at[i]) for i in range(blocks)]
    for tile_copy in tile_copies:
        tile_copy.start()
    peers = message_ref.shape[0]
    units = hidden_ref.shape[0]
    feats = term_ref.shape[1] // peers
    rows = blocks * feats
    at = 2 * rows
    me = lax.axis_index("col")
    chunk = out_ref.shape[1] - (units + 8)

    for part in range(out_ref.shape[0]):
        out_ref[part, :chunk, :] = jnp.zeros((chunk, tile), F32)
    weight = jnp.concatenate([message_ref[p, at:at + units, :] for p in range(peers)], axis=0)
    eye = lax.broadcasted_iota(jnp.int32, (units, tile), 0) == lax.broadcasted_iota(jnp.int32, (units, tile), 1)
    bias = jnp.concatenate(
        [
            jnp.sum(jnp.where(eye, message_ref[p, at + units:, :][:1].astype(F32), 0.0), axis=1, keepdims=True)
            for p in range(peers)
        ],
        axis=0,
    )
    weight_sum = jnp.zeros((units, peers * feats), F32)
    bias_sum = jnp.zeros((8, units), F32)
    ones = jnp.ones((8, tile), BF16)
    mine = pl.ds(pl.multiple_of(me * units, units), units)
    mine_rows = pl.ds(pl.multiple_of(me * feats, feats), feats)
    terms = []
    for i in range(blocks):
        high = jnp.concatenate([message_ref[p, i * feats:(i + 1) * feats, :] for p in range(peers)], axis=0)
        low = jnp.concatenate([message_ref[p, rows + i * feats:rows + (i + 1) * feats, :] for p in range(peers)], axis=0)
        cotangent = cotangent_ref[:, i * tile:(i + 1) * tile].astype(F32)
        pre_act = mm(weight, high) + mm(weight, low) + bias
        gate = 1.0 / (1.0 + jnp.exp(-pre_act))
        silu_ref[...] = pre_act * gate
        hidden_ref[:, i * tile:(i + 1) * tile] = silu_ref[mine, :].astype(BF16)
        grad_pre = cotangent * gate * (1.0 + pre_act * (1.0 - gate))
        grad_ref[...] = grad_pre
        grad_high, grad_low = split2(grad_pre)
        term_ref[i] = mm(weight, grad_high, 0, 0) + mm(weight, grad_low, 0, 0)
        own_high, own_low = split2(grad_ref[mine, :])
        weight_sum = weight_sum + mm(own_high, high, 1, 1) + (mm(own_high, low, 1, 1) + mm(own_low, high, 1, 1))
        bias_sum = bias_sum + mm(ones, own_high, 1, 1) + mm(ones, own_low, 1, 1)
        terms.append(jnp.concatenate(split2(term_ref[i, mine_rows, :]), axis=0))

    bias_wide = jnp.concatenate([bias_sum, jnp.zeros((8, tile - units), F32)], axis=1)
    for part in range(out_ref.shape[0]):
        out_ref[part, chunk:chunk + units, :] = weight_sum
        out_ref[part, chunk + units:, :] = bias_wide

    for i in range(blocks):
        tiles_ref = all_ref.at[i]
        tile_copies[i].wait()
        count = counts_ref[i]
        left = terms[i]
        groups = lax.div(count + (GROUP - 1), GROUP)

        def body(g, carry, i=i, count=count, left=left, tiles_ref=tiles_ref):
            first = g * GROUP
            product = mm(left, jnp.concatenate([tiles_ref[first + u] for u in range(GROUP)], axis=1))
            for u in range(GROUP):
                slot = first + u
                block = coords_ref[i, slot]
                owner = lax.div(block, blocks)
                offset = lax.div(owner, INNER) * rows + lax.rem(block, blocks) * feats
                value = product[:feats, u * tile:(u + 1) * tile] + product[feats:, u * tile:(u + 1) * tile]
                value = jnp.where(slot < count, value, 0.0)
                where = pl.ds(pl.multiple_of(offset, feats), feats)
                part = lax.rem(owner, INNER)
                out_ref[part, where, :] = out_ref[part, where, :] + value
            return carry

        lax.fori_loop(0, groups, body, 0)


def middle_kernel(in_ref, out_ref):
    peers, width, _ = out_ref.shape
    count = in_ref.shape[0]
    extra = (peers * width - in_ref.shape[1]) // (peers - 1)
    rows = width - extra
    shared = functools.reduce(lambda a, b: a + b, [in_ref[s, peers * rows:, :] for s in range(count)])
    for p in range(peers):
        part = functools.reduce(lambda a, b: a + b, [in_ref[s, p * rows:(p + 1) * rows, :] for s in range(count)])
        out_ref[p, :rows, :] = part
        out_ref[p, rows:, :] = shared


def final_kernel(norm_factor, in_ref, grad_ref, weight_ref, bias_ref):
    count = in_ref.shape[0]
    total = functools.reduce(lambda a, b: a + b, [in_ref[s] for s in range(count)])
    feats, nodes = grad_ref.shape
    tile = total.shape[1]
    blocks = nodes // tile
    for i in range(blocks):
        grad_ref[:, i * tile:(i + 1) * tile] = total[i * feats:(i + 1) * feats]
    rows = blocks * feats
    units = weight_ref.shape[0]
    weight_ref[...] = total[rows:rows + units] * norm_factor
    bias_ref[...] = total[rows + units:rows + units + 1, :units] * norm_factor


def call(kernel, out_shape, inputs, specs, scratch=(), vmem=40 << 20):
    return pl.pallas_call(
        kernel,
        out_shape=out_shape,
        in_specs=[SPECS[c] for c in specs],
        out_specs=jax.tree.map(lambda _: VMEM, out_shape),
        scratch_shapes=scratch,
        compiler_params=pltpu.CompilerParams(vmem_limit_bytes=vmem),
    )(*inputs)


def per_device(row_size, col_size, features, order, weight, bias, tiles, coords, counts, grad_hidden):
    feats, nodes = features.shape
    units = weight.shape[1]
    blocks, slots, tile, _ = tiles.shape
    rows = blocks * feats
    outer = row_size // INNER
    norm_factor = 1.0 / math.sqrt(nodes * row_size)
    inner_groups = [[q * INNER + x for x in range(INNER)] for q in range(outer)]
    outer_groups = [[q * INNER + x for q in range(outer)] for x in range(INNER)]
    spread = call(
        reorder_kernel,
        jax.ShapeDtypeStruct((row_size, rows, tile), BF16),
        (order.reshape(1, nodes), features),
        "hh",
        scratch=[pltpu.VMEM((1, nodes), jnp.int32), pltpu.VMEM(features.shape, BF16), pltpu.SemaphoreType.DMA((2,))],
        vmem=SMALL_VMEM,
    )
    everywhere = lax.all_to_all(spread, "row", 0, 0, tiled=True)
    cotangent = lax.all_gather(grad_hidden, "col", axis=0, tiled=True)
    everywhere, cotangent = lax.optimization_barrier((everywhere, cotangent))
    source = everywhere.reshape(row_size * blocks, feats, tile)
    message = call(
        forward_kernel,
        jax.ShapeDtypeStruct((col_size, 2 * rows + units + 16, tile), BF16),
        (coords, counts, source, weight.T, bias.reshape(1, units), tiles[:1], tiles),
        "ssvvvvh",
        scratch=[pltpu.VMEM((blocks - 1,) + tiles.shape[1:], BF16), pltpu.SemaphoreType.DMA],
        vmem=TILE_VMEM,
    )
    message = lax.all_to_all(message, "col", 0, 0, tiled=True)
    chunk = outer * rows
    hidden, partial = call(
        backward_kernel,
        (
            jax.ShapeDtypeStruct((units, nodes), BF16),
            jax.ShapeDtypeStruct((INNER, chunk + units + 8, tile), F32),
        ),
        (coords, counts, message, cotangent, tiles),
        "ssvvh",
        scratch=[
            pltpu.VMEM(tiles.shape, BF16),
            pltpu.VMEM((units * col_size, tile), F32),
            pltpu.VMEM((units * col_size, tile), F32),
            pltpu.VMEM((blocks, feats * col_size, tile), F32),
            pltpu.SemaphoreType.DMA((blocks,)),
        ],
        vmem=TILE_VMEM,
    )
    partial = lax.all_to_all(partial, "row", 0, 0, tiled=True, axis_index_groups=inner_groups)
    second = call(middle_kernel, jax.ShapeDtypeStruct((outer, rows + units + 8, tile), F32), (partial,), "v")
    second = lax.all_to_all(second, "row", 0, 0, tiled=True, axis_index_groups=outer_groups)
    grad_features, grad_weight, grad_bias = call(
        functools.partial(final_kernel, norm_factor),
        (
            jax.ShapeDtypeStruct((feats, nodes), F32),
            jax.ShapeDtypeStruct((units, tile), F32),
            jax.ShapeDtypeStruct((1, units), F32),
        ),
        (second,),
        "v",
    )
    return hidden, grad_features, grad_weight.T, grad_bias.reshape(units)


def solution(mesh):
    in_specs = (
        P("col", "row"),
        P("row"),
        P(None, "col"),
        P("col"),
        P("row", None, None, None),
        P("row", None),
        P("row"),
        P("col", "row"),
    )
    out_specs = (P("col", "row"), P("col", "row"), P(None, "col"), P("col"))
    body = functools.partial(per_device, mesh.shape["row"], mesh.shape["col"])
    return jax.shard_map(body, mesh=mesh, in_specs=in_specs, out_specs=out_specs, check_vma=False)
```

```python
import functools
import math

import jax
import jax.numpy as jnp
from jax import lax
from jax.experimental import pallas as pl
from jax.experimental.pallas import tpu as pltpu
from jax.sharding import PartitionSpec as P

INNER = 4
GROUP = 8
SMALL_VMEM = 60 << 20
TILE_VMEM = 51 << 20
F32 = jnp.float32
BF16 = jnp.bfloat16
VMEM = pl.BlockSpec(memory_space=pltpu.VMEM)
SPECS = {"v": VMEM, "s": pl.BlockSpec(memory_space=pltpu.SMEM), "h": pl.BlockSpec(memory_space=pltpu.HBM)}


def mm(a, b, ca=1, cb=0):
    return lax.dot_general(a, b, (((ca,), (cb,)), ((), ())), preferred_element_type=F32)


def split2(v):
    high = v.astype(BF16)
    return high, (v - high.astype(F32)).astype(BF16)


def reorder_kernel(order_hbm, features_hbm, out_ref, order_ref, features_ref, sems):
    pairs = ((order_hbm, order_ref), (features_hbm, features_ref))
    copies = [pltpu.make_async_copy(src, dst, sems.at[n]) for n, (src, dst) in enumerate(pairs)]
    for copy in copies:
        copy.start()
    feats, nodes = features_ref.shape
    tile = out_ref.shape[2]
    blocks = nodes // tile
    copies[0].wait()
    local = jnp.bitwise_and(order_ref[...], nodes - 1)
    source = lax.broadcasted_iota(jnp.int32, (nodes, nodes), 0)
    onehot = (source == local).astype(F32).astype(BF16)
    copies[1].wait()
    picked = mm(features_ref[...], onehot).astype(BF16)
    for peer in range(out_ref.shape[0]):
        for i in range(blocks):
            out_ref[peer, i * feats:(i + 1) * feats, :] = picked[:, i * tile:(i + 1) * tile]


def forward_kernel(coords_ref, counts_ref, source_ref, grad_ref, weight_ref, bias_ref, staged_ref, tiles_hbm, out_ref, later_ref, sem):
    blocks, slots, tile, _ = tiles_hbm.shape
    copy = pltpu.make_async_copy(tiles_hbm.at[pl.ds(1, blocks - 1)], later_ref, sem)
    copy.start()
    feats = source_ref.shape[1]
    peers = out_ref.shape[0]
    parts = []
    for i in range(blocks):
        tiles_ref = staged_ref.at[0] if i == 0 else later_ref.at[i - 1]
        if i == 1:
            copy.wait()
        count = counts_ref[i]
        groups = lax.div(count + (GROUP - 1), GROUP)

        def body(g, acc, i=i, count=count, tiles_ref=tiles_ref):
            first = g * GROUP
            left = []
            for u in range(GROUP):
                block = source_ref[coords_ref[i, first + u]]
                left.append(jnp.where(first + u < count, block, jnp.zeros_like(block)))
            left = jnp.concatenate(left, axis=1)
            right = jnp.concatenate([tiles_ref[first + u] for u in range(GROUP)], axis=1)
            return acc + mm(left, right, 1, 1)

        parts.append(lax.fori_loop(0, groups, body, jnp.zeros((feats, tile), F32)))
    rows = blocks * feats
    high, low = split2(jnp.concatenate(parts, axis=0))
    units = weight_ref.shape[0]
    grad = grad_ref[...]
    bias = jnp.concatenate([bias_ref[...].astype(F32), jnp.zeros((1, tile - units), F32)], axis=1)
    bias = jnp.broadcast_to(bias, (16, tile)).astype(BF16)
    for peer in range(peers):
        out_ref[peer, :rows, :] = high
        out_ref[peer, rows:2 * rows, :] = low
        for i in range(blocks):
            at = 2 * rows + i * units
            out_ref[peer, at:at + units, :] = grad[:, i * tile:(i + 1) * tile]
        at = 2 * rows + blocks * units
        out_ref[peer, at:at + units, :] = weight_ref[...]
        out_ref[peer, at + units:, :] = bias


def backward_kernel(
    coords_ref, counts_ref, message_ref, tiles_hbm, hidden_ref, out_ref, all_ref, silu_ref, grad_ref, term_ref, tile_sems
):
    blocks, slots, tile, _ = tiles_hbm.shape
    tile_copies = [pltpu.make_async_copy(tiles_hbm.at[i], all_ref.at[i], tile_sems.at[i]) for i in range(blocks)]
    for tile_copy in tile_copies:
        tile_copy.start()
    peers = message_ref.shape[0]
    units = hidden_ref.shape[0]
    feats = term_ref.shape[1] // peers
    rows = blocks * feats
    base = 2 * rows
    at = base + blocks * units
    me = lax.axis_index("col")
    chunk = out_ref.shape[1] - (units + 8)

    for part in range(out_ref.shape[0]):
        out_ref[part, :chunk, :] = jnp.zeros((chunk, tile), F32)
    weight = jnp.concatenate([message_ref[p, at:at + units, :] for p in range(peers)], axis=0)
    eye = lax.broadcasted_iota(jnp.int32, (units, tile), 0) == lax.broadcasted_iota(jnp.int32, (units, tile), 1)
    bias = jnp.concatenate(
        [
            jnp.sum(jnp.where(eye, message_ref[p, at + units:, :][:1].astype(F32), 0.0), axis=1, keepdims=True)
            for p in range(peers)
        ],
        axis=0,
    )
    weight_sum = jnp.zeros((units, peers * feats), F32)
    bias_sum = jnp.zeros((8, units), F32)
    ones = jnp.ones((8, tile), BF16)
    mine = pl.ds(pl.multiple_of(me * units, units), units)
    mine_rows = pl.ds(pl.multiple_of(me * feats, feats), feats)
    terms = []
    for i in range(blocks):
        high = jnp.concatenate([message_ref[p, i * feats:(i + 1) * feats, :] for p in range(peers)], axis=0)
        low = jnp.concatenate([message_ref[p, rows + i * feats:rows + (i + 1) * feats, :] for p in range(peers)], axis=0)
        cotangent = jnp.concatenate(
            [message_ref[p, base + i * units:base + (i + 1) * units, :] for p in range(peers)], axis=0
        ).astype(F32)
        pre_act = mm(weight, high) + mm(weight, low) + bias
        gate = 1.0 / (1.0 + jnp.exp(-pre_act))
        silu_ref[...] = pre_act * gate
        hidden_ref[:, i * tile:(i + 1) * tile] = silu_ref[mine, :].astype(BF16)
        grad_pre = cotangent * gate * (1.0 + pre_act * (1.0 - gate))
        grad_ref[...] = grad_pre
        grad_high, grad_low = split2(grad_pre)
        term_ref[i] = mm(weight, grad_high, 0, 0) + mm(weight, grad_low, 0, 0)
        own_high, own_low = split2(grad_ref[mine, :])
        weight_sum = weight_sum + mm(own_high, high, 1, 1) + (mm(own_high, low, 1, 1) + mm(own_low, high, 1, 1))
        bias_sum = bias_sum + mm(ones, own_high, 1, 1) + mm(ones, own_low, 1, 1)
        terms.append(jnp.concatenate(split2(term_ref[i, mine_rows, :]), axis=0))

    bias_wide = jnp.concatenate([bias_sum, jnp.zeros((8, tile - units), F32)], axis=1)
    for part in range(out_ref.shape[0]):
        out_ref[part, chunk:chunk + units, :] = weight_sum
        out_ref[part, chunk + units:, :] = bias_wide

    for i in range(blocks):
        tiles_ref = all_ref.at[i]
        tile_copies[i].wait()
        count = counts_ref[i]
        left = terms[i]
        groups = lax.div(count + (GROUP - 1), GROUP)

        def body(g, carry, i=i, count=count, left=left, tiles_ref=tiles_ref):
            first = g * GROUP
            product = mm(left, jnp.concatenate([tiles_ref[first + u] for u in range(GROUP)], axis=1))
            for u in range(GROUP):
                slot = first + u
                block = coords_ref[i, slot]
                owner = lax.div(block, blocks)
                offset = lax.div(owner, INNER) * rows + lax.rem(block, blocks) * feats
                value = product[:feats, u * tile:(u + 1) * tile] + product[feats:, u * tile:(u + 1) * tile]
                value = jnp.where(slot < count, value, 0.0)
                where = pl.ds(pl.multiple_of(offset, feats), feats)
                part = lax.rem(owner, INNER)
                out_ref[part, where, :] = out_ref[part, where, :] + value
            return carry

        lax.fori_loop(0, groups, body, 0)


def middle_kernel(in_ref, out_ref):
    peers, width, _ = out_ref.shape
    count = in_ref.shape[0]
    extra = (peers * width - in_ref.shape[1]) // (peers - 1)
    rows = width - extra
    shared = functools.reduce(lambda a, b: a + b, [in_ref[s, peers * rows:, :] for s in range(count)])
    for p in range(peers):
        part = functools.reduce(lambda a, b: a + b, [in_ref[s, p * rows:(p + 1) * rows, :] for s in range(count)])
        out_ref[p, :rows, :] = part
        out_ref[p, rows:, :] = shared


def final_kernel(norm_factor, in_ref, grad_ref, weight_ref, bias_ref):
    count = in_ref.shape[0]
    total = functools.reduce(lambda a, b: a + b, [in_ref[s] for s in range(count)])
    feats, nodes = grad_ref.shape
    tile = total.shape[1]
    blocks = nodes // tile
    for i in range(blocks):
        grad_ref[:, i * tile:(i + 1) * tile] = total[i * feats:(i + 1) * feats]
    rows = blocks * feats
    units = weight_ref.shape[0]
    weight_ref[...] = total[rows:rows + units] * norm_factor
    bias_ref[...] = total[rows + units:rows + units + 1, :units] * norm_factor


def call(kernel, out_shape, inputs, specs, scratch=(), vmem=40 << 20):
    return pl.pallas_call(
        kernel,
        out_shape=out_shape,
        in_specs=[SPECS[c] for c in specs],
        out_specs=jax.tree.map(lambda _: VMEM, out_shape),
        scratch_shapes=scratch,
        compiler_params=pltpu.CompilerParams(vmem_limit_bytes=vmem),
    )(*inputs)


def per_device(row_size, col_size, features, order, weight, bias, tiles, coords, counts, grad_hidden):
    feats, nodes = features.shape
    units = weight.shape[1]
    blocks, slots, tile, _ = tiles.shape
    rows = blocks * feats
    outer = row_size // INNER
    norm_factor = 1.0 / math.sqrt(nodes * row_size)
    inner_groups = [[q * INNER + x for x in range(INNER)] for q in range(outer)]
    outer_groups = [[q * INNER + x for q in range(outer)] for x in range(INNER)]
    spread = call(
        reorder_kernel,
        jax.ShapeDtypeStruct((row_size, rows, tile), BF16),
        (order.reshape(1, nodes), features),
        "hh",
        scratch=[pltpu.VMEM((1, nodes), jnp.int32), pltpu.VMEM(features.shape, BF16), pltpu.SemaphoreType.DMA((2,))],
        vmem=SMALL_VMEM,
    )
    everywhere = lax.all_to_all(spread, "row", 0, 0, tiled=True)
    source = everywhere.reshape(row_size * blocks, feats, tile)
    message = call(
        forward_kernel,
        jax.ShapeDtypeStruct((col_size, 2 * rows + blocks * units + units + 16, tile), BF16),
        (coords, counts, source, grad_hidden, weight.T, bias.reshape(1, units), tiles[:1], tiles),
        "ssvvvvvh",
        scratch=[pltpu.VMEM((blocks - 1,) + tiles.shape[1:], BF16), pltpu.SemaphoreType.DMA],
        vmem=TILE_VMEM,
    )
    message = lax.all_to_all(message, "col", 0, 0, tiled=True)
    chunk = outer * rows
    hidden, partial = call(
        backward_kernel,
        (
            jax.ShapeDtypeStruct((units, nodes), BF16),
            jax.ShapeDtypeStruct((INNER, chunk + units + 8, tile), F32),
        ),
        (coords, counts, message, tiles),
        "ssvh",
        scratch=[
            pltpu.VMEM(tiles.shape, BF16),
            pltpu.VMEM((units * col_size, tile), F32),
            pltpu.VMEM((units * col_size, tile), F32),
            pltpu.VMEM((blocks, feats * col_size, tile), F32),
            pltpu.SemaphoreType.DMA((blocks,)),
        ],
        vmem=TILE_VMEM,
    )
    partial = lax.all_to_all(partial, "row", 0, 0, tiled=True, axis_index_groups=inner_groups)
    second = call(middle_kernel, jax.ShapeDtypeStruct((outer, rows + units + 8, tile), F32), (partial,), "v")
    second = lax.all_to_all(second, "row", 0, 0, tiled=True, axis_index_groups=outer_groups)
    grad_features, grad_weight, grad_bias = call(
        functools.partial(final_kernel, norm_factor),
        (
            jax.ShapeDtypeStruct((feats, nodes), F32),
            jax.ShapeDtypeStruct((units, tile), F32),
            jax.ShapeDtypeStruct((1, units), F32),
        ),
        (second,),
        "v",
    )
    return hidden, grad_features, grad_weight.T, grad_bias.reshape(units)


def solution(mesh):
    in_specs = (
        P("col", "row"),
        P("row"),
        P(None, "col"),
        P("col"),
        P("row", None, None, None),
        P("row", None),
        P("row"),
        P("col", "row"),
    )
    out_specs = (P("col", "row"), P("col", "row"), P(None, "col"), P("col"))
    body = functools.partial(per_device, mesh.shape["row"], mesh.shape["col"])
    return jax.shard_map(body, mesh=mesh, in_specs=in_specs, out_specs=out_specs, check_vma=False)
```

```python
import functools
import math

import jax
import jax.numpy as jnp
from jax import lax
from jax.experimental import pallas as pl
from jax.experimental.pallas import tpu as pltpu
from jax.sharding import PartitionSpec as P

INNER = 4
GROUP = 8
SMALL_VMEM = 60 << 20
TILE_VMEM = 51 << 20
F32 = jnp.float32
BF16 = jnp.bfloat16
VMEM = pl.BlockSpec(memory_space=pltpu.VMEM)
SPECS = {"v": VMEM, "s": pl.BlockSpec(memory_space=pltpu.SMEM), "h": pl.BlockSpec(memory_space=pltpu.HBM)}


def mm(a, b, ca=1, cb=0):
    return lax.dot_general(a, b, (((ca,), (cb,)), ((), ())), preferred_element_type=F32)


def split2(v):
    high = v.astype(BF16)
    return high, (v - high.astype(F32)).astype(BF16)


def reorder_kernel(order_hbm, features_hbm, out_ref, order_ref, features_ref, sems):
    pairs = ((order_hbm, order_ref), (features_hbm, features_ref))
    copies = [pltpu.make_async_copy(src, dst, sems.at[n]) for n, (src, dst) in enumerate(pairs)]
    for copy in copies:
        copy.start()
    feats, nodes = features_ref.shape
    tile = out_ref.shape[2]
    blocks = nodes // tile
    copies[0].wait()
    local = jnp.bitwise_and(order_ref[...], nodes - 1)
    source = lax.broadcasted_iota(jnp.int32, (nodes, nodes), 0)
    onehot = (source == local).astype(F32).astype(BF16)
    copies[1].wait()
    picked = mm(features_ref[...], onehot).astype(BF16)
    for peer in range(out_ref.shape[0]):
        for i in range(blocks):
            out_ref[peer, i * feats:(i + 1) * feats, :] = picked[:, i * tile:(i + 1) * tile]


def forward_kernel(coords_ref, counts_ref, source_ref, grad_ref, weight_ref, bias_ref, staged_ref, tiles_hbm, out_ref, later_ref, sem):
    blocks, slots, tile, _ = tiles_hbm.shape
    copy = pltpu.make_async_copy(tiles_hbm.at[pl.ds(1, blocks - 1)], later_ref, sem)
    copy.start()
    feats = source_ref.shape[1]
    peers = out_ref.shape[0]
    parts = []
    for i in range(blocks):
        tiles_ref = staged_ref.at[0] if i == 0 else later_ref.at[i - 1]
        if i == 1:
            copy.wait()
        count = counts_ref[i]
        groups = lax.div(count + (GROUP - 1), GROUP)

        def body(g, acc, i=i, count=count, tiles_ref=tiles_ref):
            first = g * GROUP
            left = []
            for u in range(GROUP):
                block = source_ref[coords_ref[i, first + u]]
                left.append(jnp.where(first + u < count, block, jnp.zeros_like(block)))
            left = jnp.concatenate(left, axis=1)
            right = jnp.concatenate([tiles_ref[first + u] for u in range(GROUP)], axis=1)
            return acc + mm(left, right, 1, 1)

        parts.append(lax.fori_loop(0, groups, body, jnp.zeros((feats, tile), F32)))
    rows = blocks * feats
    high, low = split2(jnp.concatenate(parts, axis=0))
    units = weight_ref.shape[0]
    grad = grad_ref[...]
    bias = jnp.concatenate([bias_ref[...].astype(F32), jnp.zeros((1, tile - units), F32)], axis=1)
    bias = jnp.broadcast_to(bias, (16, tile)).astype(BF16)
    for peer in range(peers):
        out_ref[peer, :rows, :] = high
        out_ref[peer, rows:2 * rows, :] = low
        for i in range(blocks):
            at = 2 * rows + i * units
            out_ref[peer, at:at + units, :] = grad[:, i * tile:(i + 1) * tile]
        at = 2 * rows + blocks * units
        out_ref[peer, at:at + units, :] = weight_ref[...]
        out_ref[peer, at + units:, :] = bias


def backward_kernel(
    coords_ref, counts_ref, message_ref, tiles_hbm, hidden_ref, out_ref, all_ref, silu_ref, grad_ref, term_ref, tile_sems
):
    blocks, slots, tile, _ = tiles_hbm.shape
    tile_copies = [pltpu.make_async_copy(tiles_hbm.at[i], all_ref.at[i], tile_sems.at[i]) for i in range(blocks)]
    for tile_copy in tile_copies:
        tile_copy.start()
    peers = message_ref.shape[0]
    units = hidden_ref.shape[0]
    feats = term_ref.shape[1] // peers
    rows = blocks * feats
    base = 2 * rows
    at = base + blocks * units
    me = lax.axis_index("col")
    chunk = out_ref.shape[1] - (units + 8)

    for part in range(out_ref.shape[0]):
        out_ref[part, :chunk, :] = jnp.zeros((chunk, tile), F32)
    weight = jnp.concatenate([message_ref[p, at:at + units, :] for p in range(peers)], axis=0)
    eye = lax.broadcasted_iota(jnp.int32, (units, tile), 0) == lax.broadcasted_iota(jnp.int32, (units, tile), 1)
    bias = jnp.concatenate(
        [
            jnp.sum(jnp.where(eye, message_ref[p, at + units:, :][:1].astype(F32), 0.0), axis=1, keepdims=True)
            for p in range(peers)
        ],
        axis=0,
    )
    weight_sum = jnp.zeros((units, peers * feats), F32)
    bias_sum = jnp.zeros((8, units), F32)
    ones = jnp.ones((8, tile), BF16)
    mine = pl.ds(pl.multiple_of(me * units, units), units)
    mine_rows = pl.ds(pl.multiple_of(me * feats, feats), feats)
    terms = []
    for i in range(blocks):
        high = jnp.concatenate([message_ref[p, i * feats:(i + 1) * feats, :] for p in range(peers)], axis=0)
        low = jnp.concatenate([message_ref[p, rows + i * feats:rows + (i + 1) * feats, :] for p in range(peers)], axis=0)
        cotangent = jnp.concatenate(
            [message_ref[p, base + i * units:base + (i + 1) * units, :] for p in range(peers)], axis=0
        ).astype(F32)
        pre_act = mm(weight, high) + mm(weight, low) + bias
        gate = 1.0 / (1.0 + jnp.exp(-pre_act))
        silu_ref[...] = pre_act * gate
        hidden_ref[:, i * tile:(i + 1) * tile] = silu_ref[mine, :].astype(BF16)
        grad_pre = cotangent * gate * (1.0 + pre_act * (1.0 - gate))
        grad_ref[...] = grad_pre
        grad_high, grad_low = split2(grad_pre)
        term_ref[i] = mm(weight, grad_high, 0, 0) + mm(weight, grad_low, 0, 0)
        own_high, own_low = split2(grad_ref[mine, :])
        weight_sum = weight_sum + mm(own_high, high, 1, 1) + (mm(own_high, low, 1, 1) + mm(own_low, high, 1, 1))
        bias_sum = bias_sum + mm(ones, own_high, 1, 1) + mm(ones, own_low, 1, 1)
        terms.append(jnp.concatenate(split2(term_ref[i, mine_rows, :]), axis=0))

    bias_wide = jnp.concatenate([bias_sum, jnp.zeros((8, tile - units), F32)], axis=1)
    for part in range(out_ref.shape[0]):
        out_ref[part, chunk:chunk + units, :] = weight_sum
        out_ref[part, chunk + units:, :] = bias_wide

    for i in range(blocks):
        tiles_ref = all_ref.at[i]
        tile_copies[i].wait()
        count = counts_ref[i]
        left = terms[i]
        groups = lax.div(count + (GROUP - 1), GROUP)

        def body(g, carry, i=i, count=count, left=left, tiles_ref=tiles_ref):
            first = g * GROUP
            product = mm(left, jnp.concatenate([tiles_ref[first + u] for u in range(GROUP)], axis=1))
            for u in range(GROUP):
                slot = first + u
                block = coords_ref[i, slot]
                owner = lax.div(block, blocks)
                offset = lax.div(owner, INNER) * rows + lax.rem(block, blocks) * feats
                value = product[:feats, u * tile:(u + 1) * tile] + product[feats:, u * tile:(u + 1) * tile]
                value = jnp.where(slot < count, value, 0.0)
                where = pl.ds(pl.multiple_of(offset, feats), feats)
                part = lax.rem(owner, INNER)
                out_ref[part, where, :] = out_ref[part, where, :] + value
            return carry

        lax.fori_loop(0, groups, body, 0)


def exponent_of(largest):
    power = 13.0 - jnp.floor(jnp.log2(jnp.maximum(largest, 1e-37)))
    return jnp.clip(power, -100.0, 100.0)


def largest_of(values):
    return jnp.max(jnp.max(jnp.abs(values), axis=0, keepdims=True), axis=1, keepdims=True)


def middle_kernel(in_ref, out_ref):
    peers, width, tile = out_ref.shape
    count, height, _ = in_ref.shape
    extra = height - peers * ((height // peers) // 16 * 16)
    rows = (height - extra) // peers
    units = width - rows - 16
    add = functools.partial(functools.reduce, lambda a, b: a + b)
    shared = add([in_ref[s, peers * rows:, :] for s in range(count)])
    largest = jnp.zeros((rows, tile), F32)
    for p in range(peers):
        part = add([in_ref[s, p * rows:(p + 1) * rows, :] for s in range(count)])
        out_ref[p, :rows, :] = part
        largest = jnp.maximum(largest, jnp.abs(part))
    powers = (exponent_of(largest_of(largest)), exponent_of(largest_of(shared)))
    scale, shared_scale = (jnp.broadcast_to(jnp.exp2(power), (1, tile)) for power in powers)
    row = lax.broadcasted_iota(jnp.int32, (8, tile), 0)
    note = jnp.where(row == 0, powers[0], jnp.where(row == 1, powers[1], 0.0))
    shared = shared * shared_scale
    for p in range(peers):
        out_ref[p, :rows, :] = out_ref[p, :rows, :] * scale
        out_ref[p, rows:rows + units + 8, :] = shared
        out_ref[p, rows + units + 8:, :] = note


def final_kernel(norm_factor, in_ref, grad_ref, weight_ref, bias_ref):
    count, width, tile = in_ref.shape
    feats, nodes = grad_ref.shape
    units = weight_ref.shape[0]
    blocks = nodes // tile
    rows = blocks * feats
    total = jnp.zeros((rows, tile), F32)
    shared = jnp.zeros((units + 8, tile), F32)
    for s in range(count):
        note = jnp.exp2(-in_ref[s, rows + units + 8:, :])
        total = total + in_ref[s, :rows, :] * note[:1]
        shared = shared + in_ref[s, rows:rows + units + 8, :] * note[1:2]
    for i in range(blocks):
        grad_ref[:, i * tile:(i + 1) * tile] = total[i * feats:(i + 1) * feats]
    weight_ref[...] = shared[:units] * norm_factor
    bias_ref[...] = shared[units:units + 1, :units] * norm_factor


def call(kernel, out_shape, inputs, specs, scratch=(), vmem=40 << 20):
    return pl.pallas_call(
        kernel,
        out_shape=out_shape,
        in_specs=[SPECS[c] for c in specs],
        out_specs=jax.tree.map(lambda _: VMEM, out_shape),
        scratch_shapes=scratch,
        compiler_params=pltpu.CompilerParams(vmem_limit_bytes=vmem),
    )(*inputs)


def per_device(row_size, col_size, features, order, weight, bias, tiles, coords, counts, grad_hidden):
    feats, nodes = features.shape
    units = weight.shape[1]
    blocks, slots, tile, _ = tiles.shape
    rows = blocks * feats
    outer = row_size // INNER
    norm_factor = 1.0 / math.sqrt(nodes * row_size)
    inner_groups = [[q * INNER + x for x in range(INNER)] for q in range(outer)]
    outer_groups = [[q * INNER + x for q in range(outer)] for x in range(INNER)]
    spread = call(
        reorder_kernel,
        jax.ShapeDtypeStruct((row_size, rows, tile), BF16),
        (order.reshape(1, nodes), features),
        "hh",
        scratch=[pltpu.VMEM((1, nodes), jnp.int32), pltpu.VMEM(features.shape, BF16), pltpu.SemaphoreType.DMA((2,))],
        vmem=SMALL_VMEM,
    )
    everywhere = lax.all_to_all(spread, "row", 0, 0, tiled=True)
    source = everywhere.reshape(row_size * blocks, feats, tile)
    message = call(
        forward_kernel,
        jax.ShapeDtypeStruct((col_size, 2 * rows + blocks * units + units + 16, tile), BF16),
        (coords, counts, source, grad_hidden, weight.T, bias.reshape(1, units), tiles[:1], tiles),
        "ssvvvvvh",
        scratch=[pltpu.VMEM((blocks - 1,) + tiles.shape[1:], BF16), pltpu.SemaphoreType.DMA],
        vmem=TILE_VMEM,
    )
    message = lax.all_to_all(message, "col", 0, 0, tiled=True)
    chunk = outer * rows
    hidden, partial = call(
        backward_kernel,
        (
            jax.ShapeDtypeStruct((units, nodes), BF16),
            jax.ShapeDtypeStruct((INNER, chunk + units + 8, tile), F32),
        ),
        (coords, counts, message, tiles),
        "ssvh",
        scratch=[
            pltpu.VMEM(tiles.shape, BF16),
            pltpu.VMEM((units * col_size, tile), F32),
            pltpu.VMEM((units * col_size, tile), F32),
            pltpu.VMEM((blocks, feats * col_size, tile), F32),
            pltpu.SemaphoreType.DMA((blocks,)),
        ],
        vmem=TILE_VMEM,
    )
    partial = lax.all_to_all(partial, "row", 0, 0, tiled=True, axis_index_groups=inner_groups)
    second = call(middle_kernel, jax.ShapeDtypeStruct((outer, rows + units + 16, tile), F32), (partial,), "v")
    second = lax.all_to_all(second.astype(jnp.float16), "row", 0, 0, tiled=True, axis_index_groups=outer_groups)
    second = second.astype(F32)
    grad_features, grad_weight, grad_bias = call(
        functools.partial(final_kernel, norm_factor),
        (
            jax.ShapeDtypeStruct((feats, nodes), F32),
            jax.ShapeDtypeStruct((units, tile), F32),
            jax.ShapeDtypeStruct((1, units), F32),
        ),
        (second,),
        "v",
    )
    return hidden, grad_features, grad_weight.T, grad_bias.reshape(units)


def solution(mesh):
    in_specs = (
        P("col", "row"),
        P("row"),
        P(None, "col"),
        P("col"),
        P("row", None, None, None),
        P("row", None),
        P("row"),
        P("col", "row"),
    )
    out_specs = (P("col", "row"), P("col", "row"), P(None, "col"), P("col"))
    body = functools.partial(per_device, mesh.shape["row"], mesh.shape["col"])
    return jax.shard_map(body, mesh=mesh, in_specs=in_specs, out_specs=out_specs, check_vma=False)
```

```python
import functools
import math

import jax
import jax.numpy as jnp
from jax import lax
from jax.experimental import pallas as pl
from jax.experimental.pallas import tpu as pltpu
from jax.sharding import PartitionSpec as P

INNER = 4
GROUP = 8
SMALL_VMEM = 60 << 20
TILE_VMEM = 51 << 20
F32 = jnp.float32
BF16 = jnp.bfloat16
VMEM = pl.BlockSpec(memory_space=pltpu.VMEM)
SPECS = {"v": VMEM, "s": pl.BlockSpec(memory_space=pltpu.SMEM), "h": pl.BlockSpec(memory_space=pltpu.HBM)}


def mm(a, b, ca=1, cb=0):
    return lax.dot_general(a, b, (((ca,), (cb,)), ((), ())), preferred_element_type=F32)


def split2(v):
    high = v.astype(BF16)
    return high, (v - high.astype(F32)).astype(BF16)


def reorder_kernel(order_hbm, features_hbm, out_ref, order_ref, features_ref, sems):
    pairs = ((order_hbm, order_ref), (features_hbm, features_ref))
    copies = [pltpu.make_async_copy(src, dst, sems.at[n]) for n, (src, dst) in enumerate(pairs)]
    for copy in copies:
        copy.start()
    feats, nodes = features_ref.shape
    tile = out_ref.shape[2]
    blocks = nodes // tile
    copies[0].wait()
    local = jnp.bitwise_and(order_ref[...], nodes - 1)
    source = lax.broadcasted_iota(jnp.int32, (nodes, nodes), 0)
    onehot = (source == local).astype(F32).astype(BF16)
    copies[1].wait()
    picked = mm(features_ref[...], onehot).astype(BF16)
    for peer in range(out_ref.shape[0]):
        for i in range(blocks):
            out_ref[peer, i * feats:(i + 1) * feats, :] = picked[:, i * tile:(i + 1) * tile]


def forward_kernel(coords_ref, counts_ref, source_ref, grad_ref, weight_ref, bias_ref, staged_ref, tiles_hbm, out_ref, later_ref, sem):
    blocks, slots, tile, _ = tiles_hbm.shape
    copy = pltpu.make_async_copy(tiles_hbm.at[pl.ds(1, blocks - 1)], later_ref, sem)
    copy.start()
    feats = source_ref.shape[1]
    peers = out_ref.shape[0]
    parts = []
    for i in range(blocks):
        tiles_ref = staged_ref.at[0] if i == 0 else later_ref.at[i - 1]
        if i == 1:
            copy.wait()
        count = counts_ref[i]
        groups = lax.div(count + (GROUP - 1), GROUP)

        def body(g, acc, i=i, count=count, tiles_ref=tiles_ref):
            first = g * GROUP
            left = []
            for u in range(GROUP):
                block = source_ref[coords_ref[i, first + u]]
                left.append(jnp.where(first + u < count, block, jnp.zeros_like(block)))
            left = jnp.concatenate(left, axis=1)
            right = jnp.concatenate([tiles_ref[first + u] for u in range(GROUP)], axis=1)
            return acc + mm(left, right, 1, 1)

        parts.append(lax.fori_loop(0, groups, body, jnp.zeros((feats, tile), F32)))
    rows = blocks * feats
    high, low = split2(jnp.concatenate(parts, axis=0))
    units = weight_ref.shape[0]
    grad = grad_ref[...]
    bias = jnp.concatenate([bias_ref[...].astype(F32), jnp.zeros((1, tile - units), F32)], axis=1)
    bias = jnp.broadcast_to(bias, (16, tile)).astype(BF16)
    for peer in range(peers):
        out_ref[peer, :rows, :] = high
        out_ref[peer, rows:2 * rows, :] = low
        for i in range(blocks):
            at = 2 * rows + i * units
            out_ref[peer, at:at + units, :] = grad[:, i * tile:(i + 1) * tile]
        at = 2 * rows + blocks * units
        out_ref[peer, at:at + units, :] = weight_ref[...]
        out_ref[peer, at + units:, :] = bias


def exponent_of(largest):
    power = 13.0 - jnp.floor(jnp.log2(jnp.maximum(largest, 1e-37)))
    return jnp.clip(power, -100.0, 100.0)


def largest_of(values):
    return jnp.max(jnp.max(jnp.abs(values), axis=0, keepdims=True), axis=1, keepdims=True)


def note_of(powers, tile):
    row = lax.broadcasted_iota(jnp.int32, (8, tile), 0)
    return jnp.where(row == 0, powers[0], jnp.where(row == 1, powers[1], 0.0))


def backward_kernel(
    coords_ref, counts_ref, message_ref, tiles_hbm, hidden_ref, out_ref, all_ref, silu_ref, grad_ref, term_ref, tile_sems
):
    blocks, slots, tile, _ = tiles_hbm.shape
    tile_copies = [pltpu.make_async_copy(tiles_hbm.at[i], all_ref.at[i], tile_sems.at[i]) for i in range(blocks)]
    for tile_copy in tile_copies:
        tile_copy.start()
    peers = message_ref.shape[0]
    units = hidden_ref.shape[0]
    feats = term_ref.shape[1] // peers
    rows = blocks * feats
    base = 2 * rows
    at = base + blocks * units
    me = lax.axis_index("col")
    chunk = out_ref.shape[1] - (units + 16)

    for part in range(out_ref.shape[0]):
        out_ref[part, :chunk, :] = jnp.zeros((chunk, tile), F32)
    weight = jnp.concatenate([message_ref[p, at:at + units, :] for p in range(peers)], axis=0)
    eye = lax.broadcasted_iota(jnp.int32, (units, tile), 0) == lax.broadcasted_iota(jnp.int32, (units, tile), 1)
    bias = jnp.concatenate(
        [
            jnp.sum(jnp.where(eye, message_ref[p, at + units:, :][:1].astype(F32), 0.0), axis=1, keepdims=True)
            for p in range(peers)
        ],
        axis=0,
    )
    weight_sum = jnp.zeros((units, peers * feats), F32)
    bias_sum = jnp.zeros((8, units), F32)
    ones = jnp.ones((8, tile), BF16)
    mine = pl.ds(pl.multiple_of(me * units, units), units)
    mine_rows = pl.ds(pl.multiple_of(me * feats, feats), feats)
    terms = []
    for i in range(blocks):
        high = jnp.concatenate([message_ref[p, i * feats:(i + 1) * feats, :] for p in range(peers)], axis=0)
        low = jnp.concatenate([message_ref[p, rows + i * feats:rows + (i + 1) * feats, :] for p in range(peers)], axis=0)
        cotangent = jnp.concatenate(
            [message_ref[p, base + i * units:base + (i + 1) * units, :] for p in range(peers)], axis=0
        ).astype(F32)
        pre_act = mm(weight, high) + mm(weight, low) + bias
        gate = 1.0 / (1.0 + jnp.exp(-pre_act))
        silu_ref[...] = pre_act * gate
        hidden_ref[:, i * tile:(i + 1) * tile] = silu_ref[mine, :].astype(BF16)
        grad_pre = cotangent * gate * (1.0 + pre_act * (1.0 - gate))
        grad_ref[...] = grad_pre
        grad_high, grad_low = split2(grad_pre)
        term_ref[i] = mm(weight, grad_high, 0, 0) + mm(weight, grad_low, 0, 0)
        own_high, own_low = split2(grad_ref[mine, :])
        weight_sum = weight_sum + mm(own_high, high, 1, 1) + (mm(own_high, low, 1, 1) + mm(own_low, high, 1, 1))
        bias_sum = bias_sum + mm(ones, own_high, 1, 1) + mm(ones, own_low, 1, 1)
        terms.append(jnp.concatenate(split2(term_ref[i, mine_rows, :]), axis=0))

    bias_wide = jnp.concatenate([bias_sum, jnp.zeros((8, tile - units), F32)], axis=1)
    for i in range(blocks):
        tiles_ref = all_ref.at[i]
        tile_copies[i].wait()
        count = counts_ref[i]
        left = terms[i]
        groups = lax.div(count + (GROUP - 1), GROUP)

        def body(g, carry, i=i, count=count, left=left, tiles_ref=tiles_ref):
            first = g * GROUP
            product = mm(left, jnp.concatenate([tiles_ref[first + u] for u in range(GROUP)], axis=1))
            for u in range(GROUP):
                slot = first + u
                block = coords_ref[i, slot]
                owner = lax.div(block, blocks)
                offset = lax.div(owner, INNER) * rows + lax.rem(block, blocks) * feats
                value = product[:feats, u * tile:(u + 1) * tile] + product[feats:, u * tile:(u + 1) * tile]
                value = jnp.where(slot < count, value, 0.0)
                where = pl.ds(pl.multiple_of(offset, feats), feats)
                part = lax.rem(owner, INNER)
                out_ref[part, where, :] = out_ref[part, where, :] + value
            return carry

        lax.fori_loop(0, groups, body, 0)

    parts = out_ref.shape[0]

    def find(n, largest):
        where = pl.ds(pl.multiple_of(n * rows, rows), rows)
        for part in range(parts):
            largest = jnp.maximum(largest, jnp.abs(out_ref[part, where, :]))
        return largest

    largest = lax.fori_loop(0, chunk // rows, find, jnp.zeros((rows, tile), F32))
    shared = jnp.concatenate([weight_sum, bias_wide], axis=0)
    powers = (exponent_of(largest_of(largest)), exponent_of(largest_of(shared)))
    scale, shared_scale = (jnp.broadcast_to(jnp.exp2(power), (1, tile)) for power in powers)

    def rescale(n, carry):
        where = pl.ds(pl.multiple_of(n * rows, rows), rows)
        for part in range(parts):
            out_ref[part, where, :] = out_ref[part, where, :] * scale
        return carry

    lax.fori_loop(0, chunk // rows, rescale, 0)
    shared = jnp.concatenate([shared * shared_scale, note_of(powers, tile)], axis=0)
    for part in range(parts):
        out_ref[part, chunk:, :] = shared


def middle_kernel(in_ref, out_ref):
    peers, width, tile = out_ref.shape
    count, height, _ = in_ref.shape
    rows = (height - width) // (peers - 1)
    units = width - rows - 16
    add = functools.partial(functools.reduce, lambda a, b: a + b)
    notes = [jnp.exp2(-in_ref[s, height - 8:, :]) for s in range(count)]
    shared = add([in_ref[s, peers * rows:height - 8, :] * notes[s][1:2] for s in range(count)])
    largest = jnp.zeros((rows, tile), F32)
    for p in range(peers):
        part = add([in_ref[s, p * rows:(p + 1) * rows, :] * notes[s][:1] for s in range(count)])
        out_ref[p, :rows, :] = part
        largest = jnp.maximum(largest, jnp.abs(part))
    powers = (exponent_of(largest_of(largest)), exponent_of(largest_of(shared)))
    scale, shared_scale = (jnp.broadcast_to(jnp.exp2(power), (1, tile)) for power in powers)
    note = note_of(powers, tile)
    shared = shared * shared_scale
    for p in range(peers):
        out_ref[p, :rows, :] = out_ref[p, :rows, :] * scale
        out_ref[p, rows:rows + units + 8, :] = shared
        out_ref[p, rows + units + 8:, :] = note


def final_kernel(norm_factor, in_ref, grad_ref, weight_ref, bias_ref):
    count, width, tile = in_ref.shape
    feats, nodes = grad_ref.shape
    units = weight_ref.shape[0]
    blocks = nodes // tile
    rows = blocks * feats
    total = jnp.zeros((rows, tile), F32)
    shared = jnp.zeros((units + 8, tile), F32)
    for s in range(count):
        note = jnp.exp2(-in_ref[s, rows + units + 8:, :])
        total = total + in_ref[s, :rows, :] * note[:1]
        shared = shared + in_ref[s, rows:rows + units + 8, :] * note[1:2]
    for i in range(blocks):
        grad_ref[:, i * tile:(i + 1) * tile] = total[i * feats:(i + 1) * feats]
    weight_ref[...] = shared[:units] * norm_factor
    bias_ref[...] = shared[units:units + 1, :units] * norm_factor


def call(kernel, out_shape, inputs, specs, scratch=(), vmem=40 << 20):
    return pl.pallas_call(
        kernel,
        out_shape=out_shape,
        in_specs=[SPECS[c] for c in specs],
        out_specs=jax.tree.map(lambda _: VMEM, out_shape),
        scratch_shapes=scratch,
        compiler_params=pltpu.CompilerParams(vmem_limit_bytes=vmem),
    )(*inputs)


def per_device(row_size, col_size, features, order, weight, bias, tiles, coords, counts, grad_hidden):
    feats, nodes = features.shape
    units = weight.shape[1]
    blocks, slots, tile, _ = tiles.shape
    rows = blocks * feats
    outer = row_size // INNER
    norm_factor = 1.0 / math.sqrt(nodes * row_size)
    inner_groups = [[q * INNER + x for x in range(INNER)] for q in range(outer)]
    outer_groups = [[q * INNER + x for q in range(outer)] for x in range(INNER)]
    spread = call(
        reorder_kernel,
        jax.ShapeDtypeStruct((row_size, rows, tile), BF16),
        (order.reshape(1, nodes), features),
        "hh",
        scratch=[pltpu.VMEM((1, nodes), jnp.int32), pltpu.VMEM(features.shape, BF16), pltpu.SemaphoreType.DMA((2,))],
        vmem=SMALL_VMEM,
    )
    everywhere = lax.all_to_all(spread, "row", 0, 0, tiled=True)
    source = everywhere.reshape(row_size * blocks, feats, tile)
    message = call(
        forward_kernel,
        jax.ShapeDtypeStruct((col_size, 2 * rows + blocks * units + units + 16, tile), BF16),
        (coords, counts, source, grad_hidden, weight.T, bias.reshape(1, units), tiles[:1], tiles),
        "ssvvvvvh",
        scratch=[pltpu.VMEM((blocks - 1,) + tiles.shape[1:], BF16), pltpu.SemaphoreType.DMA],
        vmem=TILE_VMEM,
    )
    message = lax.all_to_all(message, "col", 0, 0, tiled=True)
    chunk = outer * rows
    hidden, partial = call(
        backward_kernel,
        (
            jax.ShapeDtypeStruct((units, nodes), BF16),
            jax.ShapeDtypeStruct((INNER, chunk + units + 16, tile), F32),
        ),
        (coords, counts, message, tiles),
        "ssvh",
        scratch=[
            pltpu.VMEM(tiles.shape, BF16),
            pltpu.VMEM((units * col_size, tile), F32),
            pltpu.VMEM((units * col_size, tile), F32),
            pltpu.VMEM((blocks, feats * col_size, tile), F32),
            pltpu.SemaphoreType.DMA((blocks,)),
        ],
        vmem=TILE_VMEM,
    )
    partial = lax.all_to_all(partial.astype(jnp.float16), "row", 0, 0, tiled=True, axis_index_groups=inner_groups)
    partial = partial.astype(F32)
    second = call(middle_kernel, jax.ShapeDtypeStruct((outer, rows + units + 16, tile), F32), (partial,), "v")
    second = lax.all_to_all(second.astype(jnp.float16), "row", 0, 0, tiled=True, axis_index_groups=outer_groups)
    second = second.astype(F32)
    grad_features, grad_weight, grad_bias = call(
        functools.partial(final_kernel, norm_factor),
        (
            jax.ShapeDtypeStruct((feats, nodes), F32),
            jax.ShapeDtypeStruct((units, tile), F32),
            jax.ShapeDtypeStruct((1, units), F32),
        ),
        (second,),
        "v",
    )
    return hidden, grad_features, grad_weight.T, grad_bias.reshape(units)


def solution(mesh):
    in_specs = (
        P("col", "row"),
        P("row"),
        P(None, "col"),
        P("col"),
        P("row", None, None, None),
        P("row", None),
        P("row"),
        P("col", "row"),
    )
    out_specs = (P("col", "row"), P("col", "row"), P(None, "col"), P("col"))
    body = functools.partial(per_device, mesh.shape["row"], mesh.shape["col"])
    return jax.shard_map(body, mesh=mesh, in_specs=in_specs, out_specs=out_specs, check_vma=False)
```

```python
import functools
import math

import jax
import jax.numpy as jnp
from jax import lax
from jax.experimental import pallas as pl
from jax.experimental.pallas import tpu as pltpu
from jax.sharding import PartitionSpec as P

INNER = 4
GROUP = 8
PIECES = 4
SMALL_VMEM = 60 << 20
TILE_VMEM = 51 << 20
F32 = jnp.float32
BF16 = jnp.bfloat16
VMEM = pl.BlockSpec(memory_space=pltpu.VMEM)
SPECS = {"v": VMEM, "s": pl.BlockSpec(memory_space=pltpu.SMEM), "h": pl.BlockSpec(memory_space=pltpu.HBM)}


def mm(a, b, ca=1, cb=0):
    return lax.dot_general(a, b, (((ca,), (cb,)), ((), ())), preferred_element_type=F32)


def split2(v):
    high = v.astype(BF16)
    return high, (v - high.astype(F32)).astype(BF16)


def reorder_kernel(order_hbm, features_hbm, out_ref, order_ref, features_ref, sems):
    pairs = ((order_hbm, order_ref), (features_hbm, features_ref))
    copies = [pltpu.make_async_copy(src, dst, sems.at[n]) for n, (src, dst) in enumerate(pairs)]
    for copy in copies:
        copy.start()
    feats, nodes = features_ref.shape
    tile = out_ref.shape[2]
    blocks = nodes // tile
    copies[0].wait()
    local = jnp.bitwise_and(order_ref[...], nodes - 1)
    source = lax.broadcasted_iota(jnp.int32, (nodes, nodes), 0)
    onehot = (source == local).astype(F32).astype(BF16)
    copies[1].wait()
    picked = mm(features_ref[...], onehot).astype(BF16)
    for peer in range(out_ref.shape[0]):
        for i in range(blocks):
            out_ref[peer, i * feats:(i + 1) * feats, :] = picked[:, i * tile:(i + 1) * tile]


def tile_copies(tiles_hbm, later_ref, sems):
    size = later_ref.shape[1] // PIECES
    skip = tiles_hbm.shape[0] - later_ref.shape[0]
    copies = [None] * skip
    for i in range(later_ref.shape[0]):
        wheres = [pl.ds(n * size, size) for n in range(PIECES)]
        copies.append(
            [
                pltpu.make_async_copy(tiles_hbm.at[i + skip, where], later_ref.at[i, where], sems.at[i, n])
                for n, where in enumerate(wheres)
            ]
        )
    return copies


def over_groups(i, groups, slots, copies, body, carry):
    if copies[i] is None:
        return lax.fori_loop(0, groups, body, carry)
    size = slots // PIECES // GROUP
    for n in range(PIECES):
        copies[i][n].wait()
        last = jnp.minimum(groups, (n + 1) * size)
        carry = lax.fori_loop(n * size, jnp.maximum(last, n * size), body, carry)
    return carry


def forward_kernel(coords_ref, counts_ref, source_ref, grad_ref, weight_ref, bias_ref, staged_ref, tiles_hbm, out_ref, later_ref, sems):
    blocks, slots, tile, _ = tiles_hbm.shape
    copies = tile_copies(tiles_hbm, later_ref, sems)
    for copy in sum(copies[1:], []):
        copy.start()
    feats = source_ref.shape[1]
    peers = out_ref.shape[0]
    parts = []
    for i in range(blocks):
        tiles_ref = staged_ref.at[0] if i == 0 else later_ref.at[i - 1]
        count = counts_ref[i]
        groups = lax.div(count + (GROUP - 1), GROUP)

        def body(g, acc, i=i, count=count, tiles_ref=tiles_ref):
            first = g * GROUP
            left = []
            for u in range(GROUP):
                block = source_ref[coords_ref[i, first + u]]
                left.append(jnp.where(first + u < count, block, jnp.zeros_like(block)))
            left = jnp.concatenate(left, axis=1)
            right = jnp.concatenate([tiles_ref[first + u] for u in range(GROUP)], axis=1)
            return acc + mm(left, right, 1, 1)

        parts.append(over_groups(i, groups, slots, copies, body, jnp.zeros((feats, tile), F32)))
    rows = blocks * feats
    high, low = split2(jnp.concatenate(parts, axis=0))
    units = weight_ref.shape[0]
    grad = grad_ref[...]
    bias = jnp.concatenate([bias_ref[...].astype(F32), jnp.zeros((1, tile - units), F32)], axis=1)
    bias = jnp.broadcast_to(bias, (16, tile)).astype(BF16)
    for peer in range(peers):
        out_ref[peer, :rows, :] = high
        out_ref[peer, rows:2 * rows, :] = low
        for i in range(blocks):
            at = 2 * rows + i * units
            out_ref[peer, at:at + units, :] = grad[:, i * tile:(i + 1) * tile]
        at = 2 * rows + blocks * units
        out_ref[peer, at:at + units, :] = weight_ref[...]
        out_ref[peer, at + units:, :] = bias


def exponent_of(largest):
    power = 13.0 - jnp.floor(jnp.log2(jnp.maximum(largest, 1e-37)))
    return jnp.clip(power, -100.0, 100.0)


def largest_of(values):
    return jnp.max(jnp.max(jnp.abs(values), axis=0, keepdims=True), axis=1, keepdims=True)


def note_of(powers, tile):
    row = lax.broadcasted_iota(jnp.int32, (8, tile), 0)
    return jnp.where(row == 0, powers[0], jnp.where(row == 1, powers[1], 0.0))


def backward_kernel(
    coords_ref, counts_ref, message_ref, tiles_hbm, hidden_ref, out_ref, later_ref, silu_ref, grad_ref, term_ref, sems
):
    blocks, slots, tile, _ = tiles_hbm.shape
    copies = tile_copies(tiles_hbm, later_ref, sems)
    for copy in sum(copies, []):
        copy.start()
    peers = message_ref.shape[0]
    units = hidden_ref.shape[0]
    feats = term_ref.shape[1] // peers
    rows = blocks * feats
    base = 2 * rows
    at = base + blocks * units
    me = lax.axis_index("col")
    chunk = out_ref.shape[1] - (units + 16)

    for part in range(out_ref.shape[0]):
        out_ref[part, :chunk, :] = jnp.zeros((chunk, tile), F32)
    weight = jnp.concatenate([message_ref[p, at:at + units, :] for p in range(peers)], axis=0)
    eye = lax.broadcasted_iota(jnp.int32, (units, tile), 0) == lax.broadcasted_iota(jnp.int32, (units, tile), 1)
    bias = jnp.concatenate(
        [
            jnp.sum(jnp.where(eye, message_ref[p, at + units:, :][:1].astype(F32), 0.0), axis=1, keepdims=True)
            for p in range(peers)
        ],
        axis=0,
    )
    weight_sum = jnp.zeros((units, peers * feats), F32)
    bias_sum = jnp.zeros((8, units), F32)
    ones = jnp.ones((8, tile), BF16)
    mine = pl.ds(pl.multiple_of(me * units, units), units)
    mine_rows = pl.ds(pl.multiple_of(me * feats, feats), feats)
    terms = []
    for i in range(blocks):
        high = jnp.concatenate([message_ref[p, i * feats:(i + 1) * feats, :] for p in range(peers)], axis=0)
        low = jnp.concatenate([message_ref[p, rows + i * feats:rows + (i + 1) * feats, :] for p in range(peers)], axis=0)
        cotangent = jnp.concatenate(
            [message_ref[p, base + i * units:base + (i + 1) * units, :] for p in range(peers)], axis=0
        ).astype(F32)
        pre_act = mm(weight, high) + mm(weight, low) + bias
        gate = 1.0 / (1.0 + jnp.exp(-pre_act))
        silu_ref[...] = pre_act * gate
        hidden_ref[:, i * tile:(i + 1) * tile] = silu_ref[mine, :].astype(BF16)
        grad_pre = cotangent * gate * (1.0 + pre_act * (1.0 - gate))
        grad_ref[...] = grad_pre
        grad_high, grad_low = split2(grad_pre)
        term_ref[i] = mm(weight, grad_high, 0, 0) + mm(weight, grad_low, 0, 0)
        own_high, own_low = split2(grad_ref[mine, :])
        weight_sum = weight_sum + mm(own_high, high, 1, 1) + (mm(own_high, low, 1, 1) + mm(own_low, high, 1, 1))
        bias_sum = bias_sum + mm(ones, own_high, 1, 1) + mm(ones, own_low, 1, 1)
        terms.append(jnp.concatenate(split2(term_ref[i, mine_rows, :]), axis=0))

    bias_wide = jnp.concatenate([bias_sum, jnp.zeros((8, tile - units), F32)], axis=1)
    for i in range(blocks):
        tiles_ref = later_ref.at[i]
        count = counts_ref[i]
        left = terms[i]
        groups = lax.div(count + (GROUP - 1), GROUP)

        def body(g, carry, i=i, count=count, left=left, tiles_ref=tiles_ref):
            first = g * GROUP
            product = mm(left, jnp.concatenate([tiles_ref[first + u] for u in range(GROUP)], axis=1))
            for u in range(GROUP):
                slot = first + u
                block = coords_ref[i, slot]
                owner = lax.div(block, blocks)
                offset = lax.div(owner, INNER) * rows + lax.rem(block, blocks) * feats
                value = product[:feats, u * tile:(u + 1) * tile] + product[feats:, u * tile:(u + 1) * tile]
                value = jnp.where(slot < count, value, 0.0)
                where = pl.ds(pl.multiple_of(offset, feats), feats)
                part = lax.rem(owner, INNER)
                out_ref[part, where, :] = out_ref[part, where, :] + value
            return carry

        over_groups(i, groups, slots, copies, body, 0)

    parts = out_ref.shape[0]

    def find(n, largest):
        where = pl.ds(pl.multiple_of(n * rows, rows), rows)
        for part in range(parts):
            largest = jnp.maximum(largest, jnp.abs(out_ref[part, where, :]))
        return largest

    largest = lax.fori_loop(0, chunk // rows, find, jnp.zeros((rows, tile), F32))
    shared = jnp.concatenate([weight_sum, bias_wide], axis=0)
    powers = (exponent_of(largest_of(largest)), exponent_of(largest_of(shared)))
    scale, shared_scale = (jnp.broadcast_to(jnp.exp2(power), (1, tile)) for power in powers)

    def rescale(n, carry):
        where = pl.ds(pl.multiple_of(n * rows, rows), rows)
        for part in range(parts):
            out_ref[part, where, :] = out_ref[part, where, :] * scale
        return carry

    lax.fori_loop(0, chunk // rows, rescale, 0)
    shared = jnp.concatenate([shared * shared_scale, note_of(powers, tile)], axis=0)
    for part in range(parts):
        out_ref[part, chunk:, :] = shared


def middle_kernel(in_ref, out_ref):
    peers, width, tile = out_ref.shape
    count, height, _ = in_ref.shape
    rows = (height - width) // (peers - 1)
    units = width - rows - 16
    add = functools.partial(functools.reduce, lambda a, b: a + b)
    notes = [jnp.exp2(-in_ref[s, height - 8:, :]) for s in range(count)]
    shared = add([in_ref[s, peers * rows:height - 8, :] * notes[s][1:2] for s in range(count)])
    largest = jnp.zeros((rows, tile), F32)
    for p in range(peers):
        part = add([in_ref[s, p * rows:(p + 1) * rows, :] * notes[s][:1] for s in range(count)])
        out_ref[p, :rows, :] = part
        largest = jnp.maximum(largest, jnp.abs(part))
    powers = (exponent_of(largest_of(largest)), exponent_of(largest_of(shared)))
    scale, shared_scale = (jnp.broadcast_to(jnp.exp2(power), (1, tile)) for power in powers)
    note = note_of(powers, tile)
    shared = shared * shared_scale
    for p in range(peers):
        out_ref[p, :rows, :] = out_ref[p, :rows, :] * scale
        out_ref[p, rows:rows + units + 8, :] = shared
        out_ref[p, rows + units + 8:, :] = note


def final_kernel(norm_factor, in_ref, grad_ref, weight_ref, bias_ref):
    count, width, tile = in_ref.shape
    feats, nodes = grad_ref.shape
    units = weight_ref.shape[0]
    blocks = nodes // tile
    rows = blocks * feats
    total = jnp.zeros((rows, tile), F32)
    shared = jnp.zeros((units + 8, tile), F32)
    for s in range(count):
        note = jnp.exp2(-in_ref[s, rows + units + 8:, :])
        total = total + in_ref[s, :rows, :] * note[:1]
        shared = shared + in_ref[s, rows:rows + units + 8, :] * note[1:2]
    for i in range(blocks):
        grad_ref[:, i * tile:(i + 1) * tile] = total[i * feats:(i + 1) * feats]
    weight_ref[...] = shared[:units] * norm_factor
    bias_ref[...] = shared[units:units + 1, :units] * norm_factor


def call(kernel, out_shape, inputs, specs, scratch=(), vmem=40 << 20):
    return pl.pallas_call(
        kernel,
        out_shape=out_shape,
        in_specs=[SPECS[c] for c in specs],
        out_specs=jax.tree.map(lambda _: VMEM, out_shape),
        scratch_shapes=scratch,
        compiler_params=pltpu.CompilerParams(vmem_limit_bytes=vmem),
    )(*inputs)


def per_device(row_size, col_size, features, order, weight, bias, tiles, coords, counts, grad_hidden):
    feats, nodes = features.shape
    units = weight.shape[1]
    blocks, slots, tile, _ = tiles.shape
    rows = blocks * feats
    outer = row_size // INNER
    norm_factor = 1.0 / math.sqrt(nodes * row_size)
    inner_groups = [[q * INNER + x for x in range(INNER)] for q in range(outer)]
    outer_groups = [[q * INNER + x for q in range(outer)] for x in range(INNER)]
    spread = call(
        reorder_kernel,
        jax.ShapeDtypeStruct((row_size, rows, tile), BF16),
        (order.reshape(1, nodes), features),
        "hh",
        scratch=[pltpu.VMEM((1, nodes), jnp.int32), pltpu.VMEM(features.shape, BF16), pltpu.SemaphoreType.DMA((2,))],
        vmem=SMALL_VMEM,
    )
    everywhere = lax.all_to_all(spread, "row", 0, 0, tiled=True)
    source = everywhere.reshape(row_size * blocks, feats, tile)
    message = call(
        forward_kernel,
        jax.ShapeDtypeStruct((col_size, 2 * rows + blocks * units + units + 16, tile), BF16),
        (coords, counts, source, grad_hidden, weight.T, bias.reshape(1, units), tiles[:1], tiles),
        "ssvvvvvh",
        scratch=[pltpu.VMEM((blocks - 1,) + tiles.shape[1:], BF16), pltpu.SemaphoreType.DMA((blocks - 1, PIECES))],
        vmem=TILE_VMEM,
    )
    message = lax.all_to_all(message, "col", 0, 0, tiled=True)
    chunk = outer * rows
    hidden, partial = call(
        backward_kernel,
        (
            jax.ShapeDtypeStruct((units, nodes), BF16),
            jax.ShapeDtypeStruct((INNER, chunk + units + 16, tile), F32),
        ),
        (coords, counts, message, tiles),
        "ssvh",
        scratch=[
            pltpu.VMEM(tiles.shape, BF16),
            pltpu.VMEM((units * col_size, tile), F32),
            pltpu.VMEM((units * col_size, tile), F32),
            pltpu.VMEM((blocks, feats * col_size, tile), F32),
            pltpu.SemaphoreType.DMA((blocks, PIECES)),
        ],
        vmem=TILE_VMEM,
    )
    partial = lax.all_to_all(partial.astype(jnp.float16), "row", 0, 0, tiled=True, axis_index_groups=inner_groups)
    partial = partial.astype(F32)
    second = call(middle_kernel, jax.ShapeDtypeStruct((outer, rows + units + 16, tile), F32), (partial,), "v")
    second = lax.all_to_all(second.astype(jnp.float16), "row", 0, 0, tiled=True, axis_index_groups=outer_groups)
    second = second.astype(F32)
    grad_features, grad_weight, grad_bias = call(
        functools.partial(final_kernel, norm_factor),
        (
            jax.ShapeDtypeStruct((feats, nodes), F32),
            jax.ShapeDtypeStruct((units, tile), F32),
            jax.ShapeDtypeStruct((1, units), F32),
        ),
        (second,),
        "v",
    )
    return hidden, grad_features, grad_weight.T, grad_bias.reshape(units)


def solution(mesh):
    in_specs = (
        P("col", "row"),
        P("row"),
        P(None, "col"),
        P("col"),
        P("row", None, None, None),
        P("row", None),
        P("row"),
        P("col", "row"),
    )
    out_specs = (P("col", "row"), P("col", "row"), P(None, "col"), P("col"))
    body = functools.partial(per_device, mesh.shape["row"], mesh.shape["col"])
    return jax.shard_map(body, mesh=mesh, in_specs=in_specs, out_specs=out_specs, check_vma=False)
```

```python
import functools
import math

import jax
import jax.numpy as jnp
from jax import lax
from jax.experimental import pallas as pl
from jax.experimental.pallas import tpu as pltpu
from jax.sharding import PartitionSpec as P

INNER = 4
GROUP = 16
PIECES = 4
SMALL_VMEM = 60 << 20
TILE_VMEM = 51 << 20
F32 = jnp.float32
BF16 = jnp.bfloat16
VMEM = pl.BlockSpec(memory_space=pltpu.VMEM)
SPECS = {"v": VMEM, "s": pl.BlockSpec(memory_space=pltpu.SMEM), "h": pl.BlockSpec(memory_space=pltpu.HBM)}


def mm(a, b, ca=1, cb=0):
    return lax.dot_general(a, b, (((ca,), (cb,)), ((), ())), preferred_element_type=F32)


def split2(v):
    high = v.astype(BF16)
    return high, (v - high.astype(F32)).astype(BF16)


def reorder_kernel(order_hbm, features_hbm, out_ref, order_ref, features_ref, sems):
    pairs = ((order_hbm, order_ref), (features_hbm, features_ref))
    copies = [pltpu.make_async_copy(src, dst, sems.at[n]) for n, (src, dst) in enumerate(pairs)]
    for copy in copies:
        copy.start()
    feats, nodes = features_ref.shape
    tile = out_ref.shape[2]
    blocks = nodes // tile
    copies[0].wait()
    local = jnp.bitwise_and(order_ref[...], nodes - 1)
    source = lax.broadcasted_iota(jnp.int32, (nodes, nodes), 0)
    onehot = (source == local).astype(F32).astype(BF16)
    copies[1].wait()
    picked = mm(features_ref[...], onehot).astype(BF16)
    for peer in range(out_ref.shape[0]):
        for i in range(blocks):
            out_ref[peer, i * feats:(i + 1) * feats, :] = picked[:, i * tile:(i + 1) * tile]


def tile_copies(tiles_hbm, later_ref, sems):
    size = later_ref.shape[1] // PIECES
    skip = tiles_hbm.shape[0] - later_ref.shape[0]
    copies = [None] * skip
    for i in range(later_ref.shape[0]):
        wheres = [pl.ds(n * size, size) for n in range(PIECES)]
        copies.append(
            [
                pltpu.make_async_copy(tiles_hbm.at[i + skip, where], later_ref.at[i, where], sems.at[i, n])
                for n, where in enumerate(wheres)
            ]
        )
    return copies


def over_groups(i, groups, slots, copies, body, carry):
    if copies[i] is None:
        return lax.fori_loop(0, groups, body, carry)
    size = slots // PIECES // GROUP
    for n in range(PIECES):
        copies[i][n].wait()
        last = jnp.minimum(groups, (n + 1) * size)
        carry = lax.fori_loop(n * size, jnp.maximum(last, n * size), body, carry)
    return carry


def forward_kernel(coords_ref, counts_ref, source_ref, grad_ref, weight_ref, bias_ref, staged_ref, tiles_hbm, out_ref, later_ref, sems):
    blocks, slots, tile, _ = tiles_hbm.shape
    copies = tile_copies(tiles_hbm, later_ref, sems)
    for copy in sum(copies[1:], []):
        copy.start()
    feats = source_ref.shape[1]
    peers = out_ref.shape[0]
    parts = []
    for i in range(blocks):
        tiles_ref = staged_ref.at[0] if i == 0 else later_ref.at[i - 1]
        count = counts_ref[i]
        groups = lax.div(count + (GROUP - 1), GROUP)

        def body(g, acc, i=i, count=count, tiles_ref=tiles_ref):
            first = g * GROUP
            left = []
            for u in range(GROUP):
                block = source_ref[coords_ref[i, first + u]]
                left.append(jnp.where(first + u < count, block, jnp.zeros_like(block)))
            left = jnp.concatenate(left, axis=1)
            right = jnp.concatenate([tiles_ref[first + u] for u in range(GROUP)], axis=1)
            return acc + mm(left, right, 1, 1)

        parts.append(over_groups(i, groups, slots, copies, body, jnp.zeros((feats, tile), F32)))
    rows = blocks * feats
    high, low = split2(jnp.concatenate(parts, axis=0))
    units = weight_ref.shape[0]
    grad = grad_ref[...]
    bias = jnp.concatenate([bias_ref[...].astype(F32), jnp.zeros((1, tile - units), F32)], axis=1)
    bias = jnp.broadcast_to(bias, (16, tile)).astype(BF16)
    for peer in range(peers):
        out_ref[peer, :rows, :] = high
        out_ref[peer, rows:2 * rows, :] = low
        for i in range(blocks):
            at = 2 * rows + i * units
            out_ref[peer, at:at + units, :] = grad[:, i * tile:(i + 1) * tile]
        at = 2 * rows + blocks * units
        out_ref[peer, at:at + units, :] = weight_ref[...]
        out_ref[peer, at + units:, :] = bias


def exponent_of(largest):
    power = 13.0 - jnp.floor(jnp.log2(jnp.maximum(largest, 1e-37)))
    return jnp.clip(power, -100.0, 100.0)


def largest_of(values):
    return jnp.max(jnp.max(jnp.abs(values), axis=0, keepdims=True), axis=1, keepdims=True)


def note_of(powers, tile):
    row = lax.broadcasted_iota(jnp.int32, (8, tile), 0)
    return jnp.where(row == 0, powers[0], jnp.where(row == 1, powers[1], 0.0))


def backward_kernel(
    coords_ref, counts_ref, message_ref, tiles_hbm, hidden_ref, out_ref, later_ref, silu_ref, grad_ref, term_ref, sems
):
    blocks, slots, tile, _ = tiles_hbm.shape
    copies = tile_copies(tiles_hbm, later_ref, sems)
    for copy in sum(copies, []):
        copy.start()
    peers = message_ref.shape[0]
    units = hidden_ref.shape[0]
    feats = term_ref.shape[1] // peers
    rows = blocks * feats
    base = 2 * rows
    at = base + blocks * units
    me = lax.axis_index("col")
    chunk = out_ref.shape[1] - (units + 16)

    for part in range(out_ref.shape[0]):
        out_ref[part, :chunk, :] = jnp.zeros((chunk, tile), F32)
    weight = jnp.concatenate([message_ref[p, at:at + units, :] for p in range(peers)], axis=0)
    eye = lax.broadcasted_iota(jnp.int32, (units, tile), 0) == lax.broadcasted_iota(jnp.int32, (units, tile), 1)
    bias = jnp.concatenate(
        [
            jnp.sum(jnp.where(eye, message_ref[p, at + units:, :][:1].astype(F32), 0.0), axis=1, keepdims=True)
            for p in range(peers)
        ],
        axis=0,
    )
    weight_sum = jnp.zeros((units, peers * feats), F32)
    bias_sum = jnp.zeros((8, units), F32)
    ones = jnp.ones((8, tile), BF16)
    mine = pl.ds(pl.multiple_of(me * units, units), units)
    mine_rows = pl.ds(pl.multiple_of(me * feats, feats), feats)
    terms = []
    for i in range(blocks):
        high = jnp.concatenate([message_ref[p, i * feats:(i + 1) * feats, :] for p in range(peers)], axis=0)
        low = jnp.concatenate([message_ref[p, rows + i * feats:rows + (i + 1) * feats, :] for p in range(peers)], axis=0)
        cotangent = jnp.concatenate(
            [message_ref[p, base + i * units:base + (i + 1) * units, :] for p in range(peers)], axis=0
        ).astype(F32)
        pre_act = mm(weight, high) + mm(weight, low) + bias
        gate = 1.0 / (1.0 + jnp.exp(-pre_act))
        silu_ref[...] = pre_act * gate
        hidden_ref[:, i * tile:(i + 1) * tile] = silu_ref[mine, :].astype(BF16)
        grad_pre = cotangent * gate * (1.0 + pre_act * (1.0 - gate))
        grad_ref[...] = grad_pre
        grad_high, grad_low = split2(grad_pre)
        term_ref[i] = mm(weight, grad_high, 0, 0) + mm(weight, grad_low, 0, 0)
        own_high, own_low = split2(grad_ref[mine, :])
        weight_sum = weight_sum + mm(own_high, high, 1, 1) + (mm(own_high, low, 1, 1) + mm(own_low, high, 1, 1))
        bias_sum = bias_sum + mm(ones, own_high, 1, 1) + mm(ones, own_low, 1, 1)
        terms.append(jnp.concatenate(split2(term_ref[i, mine_rows, :]), axis=0))

    bias_wide = jnp.concatenate([bias_sum, jnp.zeros((8, tile - units), F32)], axis=1)
    for i in range(blocks):
        tiles_ref = later_ref.at[i]
        count = counts_ref[i]
        left = terms[i]
        groups = lax.div(count + (GROUP - 1), GROUP)

        def body(g, carry, i=i, count=count, left=left, tiles_ref=tiles_ref):
            first = g * GROUP
            product = mm(left, jnp.concatenate([tiles_ref[first + u] for u in range(GROUP)], axis=1))
            for u in range(GROUP):
                slot = first + u
                block = coords_ref[i, slot]
                owner = lax.div(block, blocks)
                offset = lax.div(owner, INNER) * rows + lax.rem(block, blocks) * feats
                value = product[:feats, u * tile:(u + 1) * tile] + product[feats:, u * tile:(u + 1) * tile]
                value = jnp.where(slot < count, value, 0.0)
                where = pl.ds(pl.multiple_of(offset, feats), feats)
                part = lax.rem(owner, INNER)
                out_ref[part, where, :] = out_ref[part, where, :] + value
            return carry

        over_groups(i, groups, slots, copies, body, 0)

    parts = out_ref.shape[0]

    def find(n, largest):
        where = pl.ds(pl.multiple_of(n * rows, rows), rows)
        for part in range(parts):
            largest = jnp.maximum(largest, jnp.abs(out_ref[part, where, :]))
        return largest

    largest = lax.fori_loop(0, chunk // rows, find, jnp.zeros((rows, tile), F32))
    shared = jnp.concatenate([weight_sum, bias_wide], axis=0)
    powers = (exponent_of(largest_of(largest)), exponent_of(largest_of(shared)))
    scale, shared_scale = (jnp.broadcast_to(jnp.exp2(power), (1, tile)) for power in powers)

    def rescale(n, carry):
        where = pl.ds(pl.multiple_of(n * rows, rows), rows)
        for part in range(parts):
            out_ref[part, where, :] = out_ref[part, where, :] * scale
        return carry

    lax.fori_loop(0, chunk // rows, rescale, 0)
    shared = jnp.concatenate([shared * shared_scale, note_of(powers, tile)], axis=0)
    for part in range(parts):
        out_ref[part, chunk:, :] = shared


def middle_kernel(in_ref, out_ref):
    peers, width, tile = out_ref.shape
    count, height, _ = in_ref.shape
    rows = (height - width) // (peers - 1)
    units = width - rows - 16
    add = functools.partial(functools.reduce, lambda a, b: a + b)
    notes = [jnp.exp2(-in_ref[s, height - 8:, :]) for s in range(count)]
    shared = add([in_ref[s, peers * rows:height - 8, :] * notes[s][1:2] for s in range(count)])
    largest = jnp.zeros((rows, tile), F32)
    for p in range(peers):
        part = add([in_ref[s, p * rows:(p + 1) * rows, :] * notes[s][:1] for s in range(count)])
        out_ref[p, :rows, :] = part
        largest = jnp.maximum(largest, jnp.abs(part))
    powers = (exponent_of(largest_of(largest)), exponent_of(largest_of(shared)))
    scale, shared_scale = (jnp.broadcast_to(jnp.exp2(power), (1, tile)) for power in powers)
    note = note_of(powers, tile)
    shared = shared * shared_scale
    for p in range(peers):
        out_ref[p, :rows, :] = out_ref[p, :rows, :] * scale
        out_ref[p, rows:rows + units + 8, :] = shared
        out_ref[p, rows + units + 8:, :] = note


def final_kernel(norm_factor, in_ref, grad_ref, weight_ref, bias_ref):
    count, width, tile = in_ref.shape
    feats, nodes = grad_ref.shape
    units = weight_ref.shape[0]
    blocks = nodes // tile
    rows = blocks * feats
    total = jnp.zeros((rows, tile), F32)
    shared = jnp.zeros((units + 8, tile), F32)
    for s in range(count):
        note = jnp.exp2(-in_ref[s, rows + units + 8:, :])
        total = total + in_ref[s, :rows, :] * note[:1]
        shared = shared + in_ref[s, rows:rows + units + 8, :] * note[1:2]
    for i in range(blocks):
        grad_ref[:, i * tile:(i + 1) * tile] = total[i * feats:(i + 1) * feats]
    weight_ref[...] = shared[:units] * norm_factor
    bias_ref[...] = shared[units:units + 1, :units] * norm_factor


def call(kernel, out_shape, inputs, specs, scratch=(), vmem=40 << 20):
    return pl.pallas_call(
        kernel,
        out_shape=out_shape,
        in_specs=[SPECS[c] for c in specs],
        out_specs=jax.tree.map(lambda _: VMEM, out_shape),
        scratch_shapes=scratch,
        compiler_params=pltpu.CompilerParams(vmem_limit_bytes=vmem),
    )(*inputs)


def per_device(row_size, col_size, features, order, weight, bias, tiles, coords, counts, grad_hidden):
    feats, nodes = features.shape
    units = weight.shape[1]
    blocks, slots, tile, _ = tiles.shape
    rows = blocks * feats
    outer = row_size // INNER
    norm_factor = 1.0 / math.sqrt(nodes * row_size)
    inner_groups = [[q * INNER + x for x in range(INNER)] for q in range(outer)]
    outer_groups = [[q * INNER + x for q in range(outer)] for x in range(INNER)]
    spread = call(
        reorder_kernel,
        jax.ShapeDtypeStruct((row_size, rows, tile), BF16),
        (order.reshape(1, nodes), features),
        "hh",
        scratch=[pltpu.VMEM((1, nodes), jnp.int32), pltpu.VMEM(features.shape, BF16), pltpu.SemaphoreType.DMA((2,))],
        vmem=SMALL_VMEM,
    )
    everywhere = lax.all_to_all(spread, "row", 0, 0, tiled=True)
    source = everywhere.reshape(row_size * blocks, feats, tile)
    message = call(
        forward_kernel,
        jax.ShapeDtypeStruct((col_size, 2 * rows + blocks * units + units + 16, tile), BF16),
        (coords, counts, source, grad_hidden, weight.T, bias.reshape(1, units), tiles[:1], tiles),
        "ssvvvvvh",
        scratch=[pltpu.VMEM((blocks - 1,) + tiles.shape[1:], BF16), pltpu.SemaphoreType.DMA((blocks - 1, PIECES))],
        vmem=TILE_VMEM,
    )
    message = lax.all_to_all(message, "col", 0, 0, tiled=True)
    chunk = outer * rows
    hidden, partial = call(
        backward_kernel,
        (
            jax.ShapeDtypeStruct((units, nodes), BF16),
            jax.ShapeDtypeStruct((INNER, chunk + units + 16, tile), F32),
        ),
        (coords, counts, message, tiles),
        "ssvh",
        scratch=[
            pltpu.VMEM(tiles.shape, BF16),
            pltpu.VMEM((units * col_size, tile), F32),
            pltpu.VMEM((units * col_size, tile), F32),
            pltpu.VMEM((blocks, feats * col_size, tile), F32),
            pltpu.SemaphoreType.DMA((blocks, PIECES)),
        ],
        vmem=TILE_VMEM,
    )
    partial = lax.all_to_all(partial.astype(jnp.float16), "row", 0, 0, tiled=True, axis_index_groups=inner_groups)
    partial = partial.astype(F32)
    second = call(middle_kernel, jax.ShapeDtypeStruct((outer, rows + units + 16, tile), F32), (partial,), "v")
    second = lax.all_to_all(second.astype(jnp.float16), "row", 0, 0, tiled=True, axis_index_groups=outer_groups)
    second = second.astype(F32)
    grad_features, grad_weight, grad_bias = call(
        functools.partial(final_kernel, norm_factor),
        (
            jax.ShapeDtypeStruct((feats, nodes), F32),
            jax.ShapeDtypeStruct((units, tile), F32),
            jax.ShapeDtypeStruct((1, units), F32),
        ),
        (second,),
        "v",
    )
    return hidden, grad_features, grad_weight.T, grad_bias.reshape(units)


def solution(mesh):
    in_specs = (
        P("col", "row"),
        P("row"),
        P(None, "col"),
        P("col"),
        P("row", None, None, None),
        P("row", None),
        P("row"),
        P("col", "row"),
    )
    out_specs = (P("col", "row"), P("col", "row"), P(None, "col"), P("col"))
    body = functools.partial(per_device, mesh.shape["row"], mesh.shape["col"])
    return jax.shard_map(body, mesh=mesh, in_specs=in_specs, out_specs=out_specs, check_vma=False)
```

```python
import functools
import math

import jax
import jax.numpy as jnp
from jax import lax
from jax.experimental import pallas as pl
from jax.experimental.pallas import tpu as pltpu
from jax.sharding import PartitionSpec as P

INNER = 4
GROUP = 16
PIECES = 4
SMALL_VMEM = 60 << 20
TILE_VMEM = 51 << 20
F32 = jnp.float32
BF16 = jnp.bfloat16
VMEM = pl.BlockSpec(memory_space=pltpu.VMEM)
SPECS = {"v": VMEM, "s": pl.BlockSpec(memory_space=pltpu.SMEM), "h": pl.BlockSpec(memory_space=pltpu.HBM)}


def mm(a, b, ca=1, cb=0):
    return lax.dot_general(a, b, (((ca,), (cb,)), ((), ())), preferred_element_type=F32)


def split2(v):
    high = v.astype(BF16)
    return high, (v - high.astype(F32)).astype(BF16)


def reorder_kernel(order_hbm, features_hbm, out_ref, order_ref, features_ref, sems):
    pairs = ((order_hbm, order_ref), (features_hbm, features_ref))
    copies = [pltpu.make_async_copy(src, dst, sems.at[n]) for n, (src, dst) in enumerate(pairs)]
    for copy in copies:
        copy.start()
    feats, nodes = features_ref.shape
    tile = out_ref.shape[2]
    blocks = nodes // tile
    copies[0].wait()
    local = jnp.bitwise_and(order_ref[...], nodes - 1)
    source = lax.broadcasted_iota(jnp.int32, (nodes, nodes), 0)
    onehot = (source == local).astype(F32).astype(BF16)
    copies[1].wait()
    picked = mm(features_ref[...], onehot).astype(BF16)
    for peer in range(out_ref.shape[0]):
        for i in range(blocks):
            out_ref[peer, i * feats:(i + 1) * feats, :] = picked[:, i * tile:(i + 1) * tile]


def tile_copies(tiles_hbm, later_ref, sems):
    size = later_ref.shape[1] // PIECES
    skip = tiles_hbm.shape[0] - later_ref.shape[0]
    copies = [None] * skip
    for i in range(later_ref.shape[0]):
        wheres = [pl.ds(n * size, size) for n in range(PIECES)]
        copies.append(
            [
                pltpu.make_async_copy(tiles_hbm.at[i + skip, where], later_ref.at[i, where], sems.at[i, n])
                for n, where in enumerate(wheres)
            ]
        )
    return copies


def over_groups(i, groups, slots, copies, body, carry):
    if copies[i] is None:
        return lax.fori_loop(0, groups, body, carry)
    size = slots // PIECES // GROUP
    for n in range(PIECES):
        copies[i][n].wait()
        last = jnp.minimum(groups, (n + 1) * size)
        carry = lax.fori_loop(n * size, jnp.maximum(last, n * size), body, carry)
    return carry


def forward_kernel(coords_ref, counts_ref, source_ref, grad_ref, weight_ref, bias_ref, staged_ref, tiles_hbm, out_ref, later_ref, sems):
    blocks, slots, tile, _ = tiles_hbm.shape
    copies = tile_copies(tiles_hbm, later_ref, sems)
    for copy in sum(copies[1:], []):
        copy.start()
    feats = source_ref.shape[1]
    peers = out_ref.shape[0]
    parts = []
    for i in range(blocks):
        tiles_ref = staged_ref.at[0] if i == 0 else later_ref.at[i - 1]
        count = counts_ref[i]
        groups = lax.div(count + (GROUP - 1), GROUP)

        def body(g, acc, i=i, count=count, tiles_ref=tiles_ref):
            first = g * GROUP
            left = []
            for u in range(GROUP):
                block = source_ref[coords_ref[i, first + u]]
                left.append(jnp.where(first + u < count, block, jnp.zeros_like(block)))
            left = jnp.concatenate(left, axis=1)
            right = jnp.concatenate([tiles_ref[first + u] for u in range(GROUP)], axis=1)
            return acc + mm(left, right, 1, 1)

        parts.append(over_groups(i, groups, slots, copies, body, jnp.zeros((feats, tile), F32)))
    rows = blocks * feats
    high, low = split2(jnp.concatenate(parts, axis=0))
    units = weight_ref.shape[0]
    grad = grad_ref[...]
    bias = jnp.concatenate([bias_ref[...].astype(F32), jnp.zeros((1, tile - units), F32)], axis=1)
    bias = jnp.broadcast_to(bias, (16, tile)).astype(BF16)
    for peer in range(peers):
        out_ref[peer, :rows, :] = high
        out_ref[peer, rows:2 * rows, :] = low
        for i in range(blocks):
            at = 2 * rows + i * units
            out_ref[peer, at:at + units, :] = grad[:, i * tile:(i + 1) * tile]
        at = 2 * rows + blocks * units
        out_ref[peer, at:at + units, :] = weight_ref[...]
        out_ref[peer, at + units:, :] = bias


def exponent_of(largest):
    power = 13.0 - jnp.floor(jnp.log2(jnp.maximum(largest, 1e-37)))
    return jnp.clip(power, -100.0, 100.0)


def largest_of(values):
    return jnp.max(jnp.max(jnp.abs(values), axis=0, keepdims=True), axis=1, keepdims=True)


def note_of(powers, tile):
    row = lax.broadcasted_iota(jnp.int32, (8, tile), 0)
    return jnp.where(row == 0, powers[0], jnp.where(row == 1, powers[1], 0.0))


def backward_kernel(
    coords_ref, counts_ref, message_ref, tiles_hbm, hidden_ref, out_ref, scale_ref, later_ref, silu_ref, grad_ref, term_ref, sems
):
    blocks, slots, tile, _ = tiles_hbm.shape
    copies = tile_copies(tiles_hbm, later_ref, sems)
    for copy in sum(copies, []):
        copy.start()
    peers = message_ref.shape[0]
    units = hidden_ref.shape[0]
    feats = term_ref.shape[1] // peers
    rows = blocks * feats
    base = 2 * rows
    at = base + blocks * units
    me = lax.axis_index("col")
    chunk = out_ref.shape[1] - (units + 16)

    for part in range(out_ref.shape[0]):
        out_ref[part, :chunk, :] = jnp.zeros((chunk, tile), F32)
    weight = jnp.concatenate([message_ref[p, at:at + units, :] for p in range(peers)], axis=0)
    eye = lax.broadcasted_iota(jnp.int32, (units, tile), 0) == lax.broadcasted_iota(jnp.int32, (units, tile), 1)
    bias = jnp.concatenate(
        [
            jnp.sum(jnp.where(eye, message_ref[p, at + units:, :][:1].astype(F32), 0.0), axis=1, keepdims=True)
            for p in range(peers)
        ],
        axis=0,
    )
    weight_sum = jnp.zeros((units, peers * feats), F32)
    bias_sum = jnp.zeros((8, units), F32)
    ones = jnp.ones((8, tile), BF16)
    mine = pl.ds(pl.multiple_of(me * units, units), units)
    mine_rows = pl.ds(pl.multiple_of(me * feats, feats), feats)
    terms = []
    for i in range(blocks):
        high = jnp.concatenate([message_ref[p, i * feats:(i + 1) * feats, :] for p in range(peers)], axis=0)
        low = jnp.concatenate([message_ref[p, rows + i * feats:rows + (i + 1) * feats, :] for p in range(peers)], axis=0)
        cotangent = jnp.concatenate(
            [message_ref[p, base + i * units:base + (i + 1) * units, :] for p in range(peers)], axis=0
        ).astype(F32)
        pre_act = mm(weight, high) + mm(weight, low) + bias
        gate = 1.0 / (1.0 + jnp.exp(-pre_act))
        silu_ref[...] = pre_act * gate
        hidden_ref[:, i * tile:(i + 1) * tile] = silu_ref[mine, :].astype(BF16)
        grad_pre = cotangent * gate * (1.0 + pre_act * (1.0 - gate))
        grad_ref[...] = grad_pre
        grad_high, grad_low = split2(grad_pre)
        term_ref[i] = mm(weight, grad_high, 0, 0) + mm(weight, grad_low, 0, 0)
        own_high, own_low = split2(grad_ref[mine, :])
        weight_sum = weight_sum + mm(own_high, high, 1, 1) + (mm(own_high, low, 1, 1) + mm(own_low, high, 1, 1))
        bias_sum = bias_sum + mm(ones, own_high, 1, 1) + mm(ones, own_low, 1, 1)
        terms.append(jnp.concatenate(split2(term_ref[i, mine_rows, :]), axis=0))

    bias_wide = jnp.concatenate([bias_sum, jnp.zeros((8, tile - units), F32)], axis=1)
    for i in range(blocks):
        tiles_ref = later_ref.at[i]
        count = counts_ref[i]
        left = terms[i]
        groups = lax.div(count + (GROUP - 1), GROUP)

        def body(g, carry, i=i, count=count, left=left, tiles_ref=tiles_ref):
            first = g * GROUP
            product = mm(left, jnp.concatenate([tiles_ref[first + u] for u in range(GROUP)], axis=1))
            for u in range(GROUP):
                slot = first + u
                block = coords_ref[i, slot]
                owner = lax.div(block, blocks)
                offset = lax.div(owner, INNER) * rows + lax.rem(block, blocks) * feats
                value = product[:feats, u * tile:(u + 1) * tile] + product[feats:, u * tile:(u + 1) * tile]
                value = jnp.where(slot < count, value, 0.0)
                where = pl.ds(pl.multiple_of(offset, feats), feats)
                part = lax.rem(owner, INNER)
                out_ref[part, where, :] = out_ref[part, where, :] + value
            return carry

        over_groups(i, groups, slots, copies, body, 0)

    parts = out_ref.shape[0]

    def find(n, largest):
        where = pl.ds(pl.multiple_of(n * rows, rows), rows)
        for part in range(parts):
            largest = jnp.maximum(largest, jnp.abs(out_ref[part, where, :]))
        return largest

    largest = lax.fori_loop(0, chunk // rows, find, jnp.zeros((rows, tile), F32))
    shared = jnp.concatenate([weight_sum, bias_wide], axis=0)
    powers = (exponent_of(largest_of(largest)), exponent_of(largest_of(shared)))
    scale, shared_scale = (jnp.broadcast_to(jnp.exp2(power), (1, tile)) for power in powers)

    scale_ref[...] = jnp.broadcast_to(scale, (8, tile))
    shared = jnp.concatenate([shared * shared_scale, note_of(powers, tile)], axis=0)
    for part in range(parts):
        out_ref[part, chunk:, :] = shared


def middle_kernel(in_ref, out_ref):
    peers, width, tile = out_ref.shape
    count, height, _ = in_ref.shape
    rows = (height - width) // (peers - 1)
    units = width - rows - 16
    add = functools.partial(functools.reduce, lambda a, b: a + b)
    notes = [jnp.exp2(-in_ref[s, height - 8:, :]) for s in range(count)]
    shared = add([in_ref[s, peers * rows:height - 8, :] * notes[s][1:2] for s in range(count)])
    largest = jnp.zeros((rows, tile), F32)
    for p in range(peers):
        part = add([in_ref[s, p * rows:(p + 1) * rows, :] * notes[s][:1] for s in range(count)])
        out_ref[p, :rows, :] = part
        largest = jnp.maximum(largest, jnp.abs(part))
    powers = (exponent_of(largest_of(largest)), exponent_of(largest_of(shared)))
    scale, shared_scale = (jnp.broadcast_to(jnp.exp2(power), (1, tile)) for power in powers)
    note = note_of(powers, tile)
    shared = shared * shared_scale
    for p in range(peers):
        out_ref[p, :rows, :] = out_ref[p, :rows, :] * scale
        out_ref[p, rows:rows + units + 8, :] = shared
        out_ref[p, rows + units + 8:, :] = note


def final_kernel(norm_factor, in_ref, grad_ref, weight_ref, bias_ref):
    count, width, tile = in_ref.shape
    feats, nodes = grad_ref.shape
    units = weight_ref.shape[0]
    blocks = nodes // tile
    rows = blocks * feats
    total = jnp.zeros((rows, tile), F32)
    shared = jnp.zeros((units + 8, tile), F32)
    for s in range(count):
        note = jnp.exp2(-in_ref[s, rows + units + 8:, :])
        total = total + in_ref[s, :rows, :] * note[:1]
        shared = shared + in_ref[s, rows:rows + units + 8, :] * note[1:2]
    for i in range(blocks):
        grad_ref[:, i * tile:(i + 1) * tile] = total[i * feats:(i + 1) * feats]
    weight_ref[...] = shared[:units] * norm_factor
    bias_ref[...] = shared[units:units + 1, :units] * norm_factor


def call(kernel, out_shape, inputs, specs, scratch=(), vmem=40 << 20):
    return pl.pallas_call(
        kernel,
        out_shape=out_shape,
        in_specs=[SPECS[c] for c in specs],
        out_specs=jax.tree.map(lambda _: VMEM, out_shape),
        scratch_shapes=scratch,
        compiler_params=pltpu.CompilerParams(vmem_limit_bytes=vmem),
    )(*inputs)


def per_device(row_size, col_size, features, order, weight, bias, tiles, coords, counts, grad_hidden):
    feats, nodes = features.shape
    units = weight.shape[1]
    blocks, slots, tile, _ = tiles.shape
    rows = blocks * feats
    outer = row_size // INNER
    norm_factor = 1.0 / math.sqrt(nodes * row_size)
    inner_groups = [[q * INNER + x for x in range(INNER)] for q in range(outer)]
    outer_groups = [[q * INNER + x for q in range(outer)] for x in range(INNER)]
    spread = call(
        reorder_kernel,
        jax.ShapeDtypeStruct((row_size, rows, tile), BF16),
        (order.reshape(1, nodes), features),
        "hh",
        scratch=[pltpu.VMEM((1, nodes), jnp.int32), pltpu.VMEM(features.shape, BF16), pltpu.SemaphoreType.DMA((2,))],
        vmem=SMALL_VMEM,
    )
    everywhere = lax.all_to_all(spread, "row", 0, 0, tiled=True)
    source = everywhere.reshape(row_size * blocks, feats, tile)
    message = call(
        forward_kernel,
        jax.ShapeDtypeStruct((col_size, 2 * rows + blocks * units + units + 16, tile), BF16),
        (coords, counts, source, grad_hidden, weight.T, bias.reshape(1, units), tiles[:1], tiles),
        "ssvvvvvh",
        scratch=[pltpu.VMEM((blocks - 1,) + tiles.shape[1:], BF16), pltpu.SemaphoreType.DMA((blocks - 1, PIECES))],
        vmem=TILE_VMEM,
    )
    message = lax.all_to_all(message, "col", 0, 0, tiled=True)
    chunk = outer * rows
    hidden, partial, scale = call(
        backward_kernel,
        (
            jax.ShapeDtypeStruct((units, nodes), BF16),
            jax.ShapeDtypeStruct((INNER, chunk + units + 16, tile), F32),
            jax.ShapeDtypeStruct((8, tile), F32),
        ),
        (coords, counts, message, tiles),
        "ssvh",
        scratch=[
            pltpu.VMEM(tiles.shape, BF16),
            pltpu.VMEM((units * col_size, tile), F32),
            pltpu.VMEM((units * col_size, tile), F32),
            pltpu.VMEM((blocks, feats * col_size, tile), F32),
            pltpu.SemaphoreType.DMA((blocks, PIECES)),
        ],
        vmem=TILE_VMEM,
    )
    summed_rows = lax.broadcasted_iota(jnp.int32, partial.shape, 1) < chunk
    partial = partial * jnp.where(summed_rows, scale[0], 1.0)
    partial = lax.all_to_all(partial.astype(jnp.float16), "row", 0, 0, tiled=True, axis_index_groups=inner_groups)
    partial = partial.astype(F32)
    second = call(middle_kernel, jax.ShapeDtypeStruct((outer, rows + units + 16, tile), F32), (partial,), "v")
    second = lax.all_to_all(second.astype(jnp.float16), "row", 0, 0, tiled=True, axis_index_groups=outer_groups)
    second = second.astype(F32)
    grad_features, grad_weight, grad_bias = call(
        functools.partial(final_kernel, norm_factor),
        (
            jax.ShapeDtypeStruct((feats, nodes), F32),
            jax.ShapeDtypeStruct((units, tile), F32),
            jax.ShapeDtypeStruct((1, units), F32),
        ),
        (second,),
        "v",
    )
    return hidden, grad_features, grad_weight.T, grad_bias.reshape(units)


def solution(mesh):
    in_specs = (
        P("col", "row"),
        P("row"),
        P(None, "col"),
        P("col"),
        P("row", None, None, None),
        P("row", None),
        P("row"),
        P("col", "row"),
    )
    out_specs = (P("col", "row"), P("col", "row"), P(None, "col"), P("col"))
    body = functools.partial(per_device, mesh.shape["row"], mesh.shape["col"])
    return jax.shard_map(body, mesh=mesh, in_specs=in_specs, out_specs=out_specs, check_vma=False)
```

```python
import functools
import math

import jax
import jax.numpy as jnp
from jax import lax
from jax.experimental import pallas as pl
from jax.experimental.pallas import tpu as pltpu
from jax.sharding import PartitionSpec as P

INNER = 4
GROUP = 16
PIECES = 4
SMALL_VMEM = 60 << 20
TILE_VMEM = 51 << 20
F32 = jnp.float32
BF16 = jnp.bfloat16
VMEM = pl.BlockSpec(memory_space=pltpu.VMEM)
SPECS = {"v": VMEM, "s": pl.BlockSpec(memory_space=pltpu.SMEM), "h": pl.BlockSpec(memory_space=pltpu.HBM)}


def mm(a, b, ca=1, cb=0):
    return lax.dot_general(a, b, (((ca,), (cb,)), ((), ())), preferred_element_type=F32)


def split2(v):
    high = v.astype(BF16)
    return high, (v - high.astype(F32)).astype(BF16)


def reorder_kernel(order_hbm, features_hbm, out_ref, order_ref, features_ref, sems):
    pairs = ((order_hbm, order_ref), (features_hbm, features_ref))
    copies = [pltpu.make_async_copy(src, dst, sems.at[n]) for n, (src, dst) in enumerate(pairs)]
    for copy in copies:
        copy.start()
    feats, nodes = features_ref.shape
    tile = out_ref.shape[2]
    blocks = nodes // tile
    copies[0].wait()
    local = jnp.bitwise_and(order_ref[...], nodes - 1)
    source = lax.broadcasted_iota(jnp.int32, (nodes, nodes), 0)
    onehot = (source == local).astype(F32).astype(BF16)
    copies[1].wait()
    picked = mm(features_ref[...], onehot).astype(BF16)
    for peer in range(out_ref.shape[0]):
        for i in range(blocks):
            out_ref[peer, i * feats:(i + 1) * feats, :] = picked[:, i * tile:(i + 1) * tile]


def tile_copies(tiles_hbm, later_ref, sems):
    size = later_ref.shape[1] // PIECES
    skip = tiles_hbm.shape[0] - later_ref.shape[0]
    copies = [None] * skip
    for i in range(later_ref.shape[0]):
        wheres = [pl.ds(n * size, size) for n in range(PIECES)]
        copies.append(
            [
                pltpu.make_async_copy(tiles_hbm.at[i + skip, where], later_ref.at[i, where], sems.at[i, n])
                for n, where in enumerate(wheres)
            ]
        )
    return copies


def over_groups(i, groups, slots, copies, body, carry):
    if copies[i] is None:
        return lax.fori_loop(0, groups, body, carry)
    size = slots // PIECES // GROUP
    for n in range(PIECES):
        copies[i][n].wait()
        last = jnp.minimum(groups, (n + 1) * size)
        carry = lax.fori_loop(n * size, jnp.maximum(last, n * size), body, carry)
    return carry


def forward_kernel(coords_ref, counts_ref, source_ref, grad_ref, weight_ref, bias_ref, staged_ref, tiles_hbm, out_ref, later_ref, sems):
    blocks, slots, tile, _ = tiles_hbm.shape
    copies = tile_copies(tiles_hbm, later_ref, sems)
    for copy in sum(copies[1:], []):
        copy.start()
    feats = source_ref.shape[1]
    peers = out_ref.shape[0]
    parts = []
    for i in range(blocks):
        tiles_ref = staged_ref.at[0] if i == 0 else later_ref.at[i - 1]
        count = counts_ref[i]
        groups = lax.div(count + (GROUP - 1), GROUP)

        def body(g, acc, i=i, count=count, tiles_ref=tiles_ref):
            first = g * GROUP
            left = []
            for u in range(GROUP):
                block = source_ref[coords_ref[i, first + u]]
                left.append(jnp.where(first + u < count, block, jnp.zeros_like(block)))
            left = jnp.concatenate(left, axis=1)
            right = jnp.concatenate([tiles_ref[first + u] for u in range(GROUP)], axis=1)
            return acc + mm(left, right, 1, 1)

        parts.append(over_groups(i, groups, slots, copies, body, jnp.zeros((feats, tile), F32)))
    rows = blocks * feats
    high, low = split2(jnp.concatenate(parts, axis=0))
    units = weight_ref.shape[0]
    grad = grad_ref[...]
    bias = jnp.concatenate([bias_ref[...].astype(F32), jnp.zeros((1, tile - units), F32)], axis=1)
    bias = jnp.broadcast_to(bias, (16, tile)).astype(BF16)
    for peer in range(peers):
        out_ref[peer, :rows, :] = high
        out_ref[peer, rows:2 * rows, :] = low
        for i in range(blocks):
            at = 2 * rows + i * units
            out_ref[peer, at:at + units, :] = grad[:, i * tile:(i + 1) * tile]
        at = 2 * rows + blocks * units
        out_ref[peer, at:at + units, :] = weight_ref[...]
        out_ref[peer, at + units:, :] = bias


def exponent_of(largest):
    power = 13.0 - jnp.floor(jnp.log2(jnp.maximum(largest, 1e-37)))
    return jnp.clip(power, -100.0, 100.0)


def largest_of(values):
    return jnp.max(jnp.max(jnp.abs(values), axis=0, keepdims=True), axis=1, keepdims=True)


def note_of(powers, tile):
    row = lax.broadcasted_iota(jnp.int32, (8, tile), 0)
    return jnp.where(row == 0, powers[0], jnp.where(row == 1, powers[1], 0.0))


def backward_kernel(
    coords_ref, counts_ref, message_ref, tiles_hbm, hidden_ref, out_ref, scale_ref, later_ref, silu_ref, grad_ref, term_ref, sems
):
    blocks, slots, tile, _ = tiles_hbm.shape
    copies = tile_copies(tiles_hbm, later_ref, sems)
    for copy in sum(copies, []):
        copy.start()
    peers = message_ref.shape[0]
    units = hidden_ref.shape[0]
    feats = term_ref.shape[1] // peers
    rows = blocks * feats
    base = 2 * rows
    at = base + blocks * units
    me = lax.axis_index("col")
    chunk = out_ref.shape[1] - (units + 16)

    for part in range(out_ref.shape[0]):
        out_ref[part, :chunk, :] = jnp.zeros((chunk, tile), F32)
    weight = jnp.concatenate([message_ref[p, at:at + units, :] for p in range(peers)], axis=0)
    eye = lax.broadcasted_iota(jnp.int32, (units, tile), 0) == lax.broadcasted_iota(jnp.int32, (units, tile), 1)
    bias = jnp.concatenate(
        [
            jnp.sum(jnp.where(eye, message_ref[p, at + units:, :][:1].astype(F32), 0.0), axis=1, keepdims=True)
            for p in range(peers)
        ],
        axis=0,
    )
    weight_sum = jnp.zeros((units, peers * feats), F32)
    bias_sum = jnp.zeros((8, units), F32)
    ones = jnp.ones((8, tile), BF16)
    mine = pl.ds(pl.multiple_of(me * units, units), units)
    mine_rows = pl.ds(pl.multiple_of(me * feats, feats), feats)
    terms = []
    for i in range(blocks):
        high = jnp.concatenate([message_ref[p, i * feats:(i + 1) * feats, :] for p in range(peers)], axis=0)
        low = jnp.concatenate([message_ref[p, rows + i * feats:rows + (i + 1) * feats, :] for p in range(peers)], axis=0)
        cotangent = jnp.concatenate(
            [message_ref[p, base + i * units:base + (i + 1) * units, :] for p in range(peers)], axis=0
        ).astype(F32)
        pre_act = mm(weight, high) + mm(weight, low) + bias
        gate = 1.0 / (1.0 + jnp.exp(-pre_act))
        silu_ref[...] = pre_act * gate
        hidden_ref[:, i * tile:(i + 1) * tile] = silu_ref[mine, :].astype(BF16)
        grad_pre = cotangent * gate * (1.0 + pre_act * (1.0 - gate))
        grad_ref[...] = grad_pre
        grad_high, grad_low = split2(grad_pre)
        term_ref[i] = mm(weight, grad_high, 0, 0) + mm(weight, grad_low, 0, 0)
        own_high, own_low = split2(grad_ref[mine, :])
        weight_sum = weight_sum + mm(own_high, high, 1, 1) + (mm(own_high, low, 1, 1) + mm(own_low, high, 1, 1))
        bias_sum = bias_sum + mm(ones, own_high, 1, 1) + mm(ones, own_low, 1, 1)
        terms.append(jnp.concatenate(split2(term_ref[i, mine_rows, :]), axis=0))

    bias_wide = jnp.concatenate([bias_sum, jnp.zeros((8, tile - units), F32)], axis=1)
    for i in range(blocks):
        tiles_ref = later_ref.at[i]
        count = counts_ref[i]
        left = terms[i]
        groups = lax.div(count + (GROUP - 1), GROUP)

        def body(g, carry, i=i, count=count, left=left, tiles_ref=tiles_ref):
            first = g * GROUP
            product = mm(left, jnp.concatenate([tiles_ref[first + u] for u in range(GROUP)], axis=1))
            for u in range(GROUP):
                slot = first + u
                block = coords_ref[i, slot]
                owner = lax.div(block, blocks)
                offset = lax.div(owner, INNER) * rows + lax.rem(block, blocks) * feats
                value = product[:feats, u * tile:(u + 1) * tile] + product[feats:, u * tile:(u + 1) * tile]
                value = jnp.where(slot < count, value, 0.0)
                where = pl.ds(pl.multiple_of(offset, feats), feats)
                part = lax.rem(owner, INNER)
                out_ref[part, where, :] = out_ref[part, where, :] + value
            return carry

        over_groups(i, groups, slots, copies, body, 0)

    parts = out_ref.shape[0]

    def find(n, largest):
        where = pl.ds(pl.multiple_of(n * rows, rows), rows)
        for part in range(parts):
            largest = jnp.maximum(largest, jnp.abs(out_ref[part, where, :]))
        return largest

    largest = lax.fori_loop(0, chunk // rows, find, jnp.zeros((rows, tile), F32))
    shared = jnp.concatenate([weight_sum, bias_wide], axis=0)
    powers = (exponent_of(largest_of(largest)), exponent_of(largest_of(shared)))
    scale, shared_scale = (jnp.broadcast_to(jnp.exp2(power), (1, tile)) for power in powers)

    scale_ref[:chunk, :] = jnp.broadcast_to(scale, (chunk, tile))
    scale_ref[chunk:, :] = jnp.ones((units + 16, tile), F32)
    shared = jnp.concatenate([shared * shared_scale, note_of(powers, tile)], axis=0)
    for part in range(parts):
        out_ref[part, chunk:, :] = shared


def middle_kernel(in_ref, out_ref):
    peers, width, tile = out_ref.shape
    count, height, _ = in_ref.shape
    rows = (height - width) // (peers - 1)
    units = width - rows - 16
    add = functools.partial(functools.reduce, lambda a, b: a + b)
    notes = [jnp.exp2(-in_ref[s, height - 8:, :]) for s in range(count)]
    shared = add([in_ref[s, peers * rows:height - 8, :] * notes[s][1:2] for s in range(count)])
    largest = jnp.zeros((rows, tile), F32)
    for p in range(peers):
        part = add([in_ref[s, p * rows:(p + 1) * rows, :] * notes[s][:1] for s in range(count)])
        out_ref[p, :rows, :] = part
        largest = jnp.maximum(largest, jnp.abs(part))
    powers = (exponent_of(largest_of(largest)), exponent_of(largest_of(shared)))
    scale, shared_scale = (jnp.broadcast_to(jnp.exp2(power), (1, tile)) for power in powers)
    note = note_of(powers, tile)
    shared = shared * shared_scale
    for p in range(peers):
        out_ref[p, :rows, :] = out_ref[p, :rows, :] * scale
        out_ref[p, rows:rows + units + 8, :] = shared
        out_ref[p, rows + units + 8:, :] = note


def final_kernel(norm_factor, in_ref, grad_ref, weight_ref, bias_ref):
    count, width, tile = in_ref.shape
    feats, nodes = grad_ref.shape
    units = weight_ref.shape[0]
    blocks = nodes // tile
    rows = blocks * feats
    total = jnp.zeros((rows, tile), F32)
    shared = jnp.zeros((units + 8, tile), F32)
    for s in range(count):
        note = jnp.exp2(-in_ref[s, rows + units + 8:, :])
        total = total + in_ref[s, :rows, :] * note[:1]
        shared = shared + in_ref[s, rows:rows + units + 8, :] * note[1:2]
    for i in range(blocks):
        grad_ref[:, i * tile:(i + 1) * tile] = total[i * feats:(i + 1) * feats]
    weight_ref[...] = shared[:units] * norm_factor
    bias_ref[...] = shared[units:units + 1, :units] * norm_factor


def call(kernel, out_shape, inputs, specs, scratch=(), vmem=40 << 20):
    return pl.pallas_call(
        kernel,
        out_shape=out_shape,
        in_specs=[SPECS[c] for c in specs],
        out_specs=jax.tree.map(lambda _: VMEM, out_shape),
        scratch_shapes=scratch,
        compiler_params=pltpu.CompilerParams(vmem_limit_bytes=vmem),
    )(*inputs)


def per_device(row_size, col_size, features, order, weight, bias, tiles, coords, counts, grad_hidden):
    feats, nodes = features.shape
    units = weight.shape[1]
    blocks, slots, tile, _ = tiles.shape
    rows = blocks * feats
    outer = row_size // INNER
    norm_factor = 1.0 / math.sqrt(nodes * row_size)
    inner_groups = [[q * INNER + x for x in range(INNER)] for q in range(outer)]
    outer_groups = [[q * INNER + x for q in range(outer)] for x in range(INNER)]
    spread = call(
        reorder_kernel,
        jax.ShapeDtypeStruct((row_size, rows, tile), BF16),
        (order.reshape(1, nodes), features),
        "hh",
        scratch=[pltpu.VMEM((1, nodes), jnp.int32), pltpu.VMEM(features.shape, BF16), pltpu.SemaphoreType.DMA((2,))],
        vmem=SMALL_VMEM,
    )
    everywhere = lax.all_to_all(spread, "row", 0, 0, tiled=True)
    source = everywhere.reshape(row_size * blocks, feats, tile)
    message = call(
        forward_kernel,
        jax.ShapeDtypeStruct((col_size, 2 * rows + blocks * units + units + 16, tile), BF16),
        (coords, counts, source, grad_hidden, weight.T, bias.reshape(1, units), tiles[:1], tiles),
        "ssvvvvvh",
        scratch=[pltpu.VMEM((blocks - 1,) + tiles.shape[1:], BF16), pltpu.SemaphoreType.DMA((blocks - 1, PIECES))],
        vmem=TILE_VMEM,
    )
    message = lax.all_to_all(message, "col", 0, 0, tiled=True)
    chunk = outer * rows
    hidden, partial, scale = call(
        backward_kernel,
        (
            jax.ShapeDtypeStruct((units, nodes), BF16),
            jax.ShapeDtypeStruct((INNER, chunk + units + 16, tile), F32),
            jax.ShapeDtypeStruct((chunk + units + 16, tile), F32),
        ),
        (coords, counts, message, tiles),
        "ssvh",
        scratch=[
            pltpu.VMEM(tiles.shape, BF16),
            pltpu.VMEM((units * col_size, tile), F32),
            pltpu.VMEM((units * col_size, tile), F32),
            pltpu.VMEM((blocks, feats * col_size, tile), F32),
            pltpu.SemaphoreType.DMA((blocks, PIECES)),
        ],
        vmem=TILE_VMEM,
    )
    partial = partial * scale
    partial = lax.all_to_all(partial.astype(jnp.float16), "row", 0, 0, tiled=True, axis_index_groups=inner_groups)
    partial = partial.astype(F32)
    second = call(middle_kernel, jax.ShapeDtypeStruct((outer, rows + units + 16, tile), F32), (partial,), "v")
    second = lax.all_to_all(second.astype(jnp.float16), "row", 0, 0, tiled=True, axis_index_groups=outer_groups)
    second = second.astype(F32)
    grad_features, grad_weight, grad_bias = call(
        functools.partial(final_kernel, norm_factor),
        (
            jax.ShapeDtypeStruct((feats, nodes), F32),
            jax.ShapeDtypeStruct((units, tile), F32),
            jax.ShapeDtypeStruct((1, units), F32),
        ),
        (second,),
        "v",
    )
    return hidden, grad_features, grad_weight.T, grad_bias.reshape(units)


def solution(mesh):
    in_specs = (
        P("col", "row"),
        P("row"),
        P(None, "col"),
        P("col"),
        P("row", None, None, None),
        P("row", None),
        P("row"),
        P("col", "row"),
    )
    out_specs = (P("col", "row"), P("col", "row"), P(None, "col"), P("col"))
    body = functools.partial(per_device, mesh.shape["row"], mesh.shape["col"])
    return jax.shard_map(body, mesh=mesh, in_specs=in_specs, out_specs=out_specs, check_vma=False)
```
